128 devices in a mesh: fluid: 32 (over x, z, core), solid: 4 (over y).
Axes of the slice: x: 4, y: 4, z: 4, core: 2. Of those that a mesh axis runs over, the one named last changes fastest.
Arguments:
- flow: bfloat16 [3, 1048576, 128], P(None, ('fluid', 'solid')), may hold values from -6 to 6
- wall_motion: float32 [3, 1048576], P(None, ('fluid', 'solid')), may hold values from -6 to 6
- normal_operator: bfloat16 [128, 128], replicated, may hold values from -0.5 to 0.5
- wall_coupling: float32 [128], replicated, may hold values from -4 to 4
- wall_stencil: bfloat16 [128], replicated, may hold values from -0.5 to 0.5
- rbf_blocks: bfloat16 [8192, 128, 128], P(('fluid', 'solid')), may hold values from -0.5 to 0.5
- block_owner: int32 [8192, 1], P(('fluid', 'solid')), may hold values from 0 to 31; in each aligned block of 64 rows (0 to 63, 64 to 127, ...) at most 3 rows name the same one
- block_row: int32 [8192, 1], P(('fluid', 'solid')), may hold values from 0 to 31
- displacement: float32 [4096, 3, 128], P(('fluid', 'solid')), may hold values from -6 to 6
- stiffness: float32 [4096, 128], P(('fluid', 'solid')), may hold values from 0.5 to 4
- residual_history: float32 [64, 4096, 3, 128], P(None, ('fluid', 'solid')), may hold values from -0.03827328 to 0.03827328
- solution_history: float32 [64, 4096, 3, 128], P(None, ('fluid', 'solid')), may hold values from -6 to 6
Outputs:
- new_flow: bfloat16 [3, 1048576, 128], P(None, ('fluid', 'solid'))
- next_displacement: float32 [4096, 3, 128], P(('fluid', 'solid'))
- wall_next: float32 [3, 1048576], P(None, ('fluid', 'solid'))
- residual_norm: float32 [], replicated
The draws below stay inside these ranges and needn't reach their ends.
Inputs may be any that keep to these rules, and one draw needn't show every extreme that they name: `block_owner`: each device's 64 blocks name no owner more than 3 times, a bound that some block reaches; every owner gets some block.
All inputs are finite; a program needn't handle non-finite values.
Results may differ from the reference program's by a relative error of at most 0.0035.
The reference program's roundings to bfloat16 on the way (of `traction`) count: a program that leaves them out, or rounds other values in their place, can miss the bound.
Values may be sent and summed in bfloat16 or wider, within the bound.
A program may use at most 128 MiB of HBM per device.

```python
import math
import jax
import jax.numpy as jnp
import numpy as np
from jax import lax

NW = 128
BLOCK = 128
SW = 128
HIST = 64
SWEEPS = 4
SR = 32
FB = 64
MOST = 3
NS = 1048576
FBLOCKS = 8192
NSR = 4096
N_FLUID = 32
N_SOLID = 4


def draw_residual_history(key, part):
    entries = NSR * 3 * SW
    subkeys = jax.random.split(jax.random.fold_in(key, 71), 4)
    directions = 4
    private = jax.random.normal(subkeys[0], (HIST, entries), jnp.float32)
    weights = 0.5 ** jnp.arange(directions, dtype=jnp.float32)
    shared = jax.random.normal(subkeys[2], (directions, entries), jnp.float32)
    mixing = jax.random.normal(subkeys[3], (HIST, directions), jnp.float32) * weights[None, :]
    common = jnp.dot(mixing, shared, precision=lax.Precision.HIGHEST)
    magnitude = math.sqrt(HIST / entries)
    values = jnp.clip(magnitude * (private + common), -6.0 * magnitude, 6.0 * magnitude)
    return values.astype(jnp.float32).reshape(HIST, NSR, 3, SW)


def touch_ends(values, stream_key, smallest, high):
    longest = values.shape.index(max(values.shape))
    spots = []
    for shift in (0, 1):
        where = [jax.random.randint(jax.random.fold_in(stream_key, axis), (), 0, length) for axis, length in enumerate(values.shape)]
        where[longest] = (where[longest] + shift) % values.shape[longest]
        spots.append(tuple(where))
    return values.at[spots[0]].set(smallest).at[spots[1]].set(high)


def level_of(rng, extent, cuts, smallest, largest):
    level, own = 1.0, jax.random.fold_in(rng, 6)
    for dim, shards_of in cuts:
        steps = jnp.exp(jax.random.uniform(jax.random.fold_in(own, dim), (shards_of,), jnp.float32, smallest / len(cuts), largest / len(cuts)))
        level = level * jnp.repeat(steps, extent[dim] // shards_of).reshape([-1 if axis == dim else 1 for axis in range(len(extent))])
    return level


def deal_out(key, own, number, rows, number_of, top, bound, skew):
    order = jax.random.permutation(key, number_of)
    packed, usual = portions_of(number_of, rows * top, bound, skew, True), portions_of(number_of, rows * top, bound, skew, False)
    places = jnp.arange(number_of)

    def named(lengths, turn):
        used = int((lengths > 0).sum())
        fixed = max(1, used // 4)
        passed = fixed + (places - fixed + turn * (used - fixed)) % max(1, number_of - fixed)
        return jnp.zeros((number_of,), jnp.int32).at[order[jnp.where(places < fixed, places, passed)]].set(jnp.asarray(lengths, jnp.int32))

    lengths = jnp.where(number % 4 == 0, named(packed, number // 4), named(usual, number - number // 4 - 1))
    mixed = jax.random.permutation(jax.random.fold_in(own, 3), number_of)
    source_of, sink = mixed[0:number_of // 2 * 2:2], mixed[1:number_of // 2 * 2:2]
    room = jnp.minimum(lengths[source_of] - 1, bound - lengths[sink]) // 2
    room = jnp.where((source_of == order[0]) | (sink == order[0]) | (lengths[sink] == 0), 0, jnp.maximum(room, 0))
    passed = jax.random.randint(jax.random.fold_in(own, 4), (number_of // 2,), 0, 1 << 20) % (room + 1)
    lengths = lengths.at[source_of].add(-passed).at[sink].add(passed)
    members = jnp.searchsorted(jnp.cumsum(lengths), jnp.arange(rows * top), side="right").astype(jnp.int32)
    table = members.reshape(top, rows).T
    table = table[jax.random.permutation(jax.random.fold_in(own, 1), rows)]
    turn = jax.random.randint(jax.random.fold_in(own, 2), (rows, 1), 0, top)
    return jnp.take_along_axis(table, (jnp.arange(top)[None, :] + turn) % top, axis=1)


def portions_of(number_of, total, bound, skew, full):
    portions = [(1 << 20) // math.isqrt(rank ** skew) + 1 for rank in range(1, number_of + 1)]
    largest = bound if full else min(bound, max(-(-total // number_of), total * portions[0] // sum(portions)))
    least = 1 if total - largest >= number_of - 1 else 0
    holding, surplus = [largest] + [least] * (number_of - 1), total - largest - least * (number_of - 1)
    while surplus > 0:
        free = [i for i in range(1, number_of) if holding[i] < largest] or [i for i in range(1, number_of) if holding[i] < bound]
        pool, remaining = sum([portions[i] for i in free]), surplus
        for i in free:
            addition = min(bound - holding[i], max(1, remaining * portions[i] // pool), surplus)
            holding[i] = holding[i] + addition
            surplus = surplus - addition
    return np.array(holding)


def bell_draw(stream_key, dims, deviation, most, shards=(), held_as=jnp.bfloat16):
    result = jax.random.normal(stream_key, dims, jnp.float32) * deviation
    if len(shards) > 0:
        result = level_of(stream_key, dims, shards, -0.22, 0.18) * result
    return jnp.clip(result, min=-most, max=most).astype(held_as)


def setup_inputs(seed: int = 0) -> dict:
    splits = jax.random.split(jax.random.key(seed), 13)
    flow = bell_draw(splits[0], (3, NS, NW), 1.0, 6.0, ((1, 128),))
    wall_motion = bell_draw(splits[1], (3, NS), 1.0, 6.0, ((1, 128),), jnp.float32)
    normal_operator = bell_draw(splits[2], (NW, NW), NW ** -0.5, 0.5)
    wall_coupling = bell_draw(splits[3], (NW,), 1.0, 4.0, (), jnp.float32)
    wall_stencil = bell_draw(splits[4], (NW,), NW ** -0.5, 0.5)
    rbf_blocks = bell_draw(splits[5], (FBLOCKS, BLOCK, SW), BLOCK ** -0.5, 0.5, ((0, 128),))
    block_owner_keys = jax.random.split(jax.random.fold_in(splits[6], 1), FBLOCKS // FB)
    block_owner_turns = jax.random.permutation(jax.random.fold_in(splits[6], 3), FBLOCKS // FB)
    block_owner = jax.vmap(lambda own, number: deal_out(jax.random.fold_in(splits[6], 2), own, number, FB, N_FLUID, 1, MOST, 2))(block_owner_keys, block_owner_turns).reshape((FBLOCKS, 1))
    block_row = touch_ends(jax.random.randint(splits[7], (FBLOCKS, 1), 0, SR), jax.random.fold_in(splits[7], 1), 0, SR - 1).astype(jnp.int32)
    displacement = bell_draw(splits[8], (NSR, 3, SW), 1.0, 6.0, ((0, 128),), jnp.float32)
    stiffness = jnp.clip(jnp.exp(math.log(4.0) - 2.0794415 * jax.random.uniform(splits[9], (NSR, SW), jnp.float32) ** level_of(splits[9], (NSR, SW), ((0, 128),), -0.2, 0.2)), 0.5, 4.0)
    residual_history = draw_residual_history(jax.random.fold_in(splits[12], 71), 0)
    solution_history = bell_draw(splits[11], (HIST, NSR, 3, SW), 1.0, 6.0, ((1, 128),), jnp.float32)
    return {"flow": flow, "wall_motion": wall_motion, "normal_operator": normal_operator, "wall_coupling": wall_coupling, "wall_stencil": wall_stencil, "rbf_blocks": rbf_blocks, "block_owner": block_owner, "block_row": block_row, "displacement": displacement, "stiffness": stiffness, "residual_history": residual_history, "solution_history": solution_history}


spread_rate = 0.25

def reference(flow, wall_motion, normal_operator, wall_coupling, wall_stencil, rbf_blocks, block_owner, block_row, displacement, stiffness, residual_history, solution_history):
    field = flow.astype(jnp.float32)
    drift = jnp.dot(flow.reshape(-1, NW).astype(jnp.float32), normal_operator.astype(jnp.float32), preferred_element_type=jnp.float32).reshape(field.shape)
    padded = jnp.pad(field, ((0, 0), (1, 1), (0, 0)))
    spread = padded[:, 2:, :] + padded[:, :-2, :] - 2.0 * field
    new_flow = (field + drift + spread_rate * spread + wall_motion[:, :, None] * wall_coupling[None, None, :]).astype(jnp.bfloat16)
    traction = jnp.dot(new_flow.reshape(-1, NW).astype(jnp.float32), wall_stencil.astype(jnp.float32), preferred_element_type=jnp.float32).astype(jnp.bfloat16)
    pieces = traction.reshape(3, FBLOCKS, BLOCK).astype(jnp.float32)
    rbf = rbf_blocks.astype(jnp.float32)
    mapped = jnp.einsum('cbp,bpq->bcq', pieces, rbf)
    home = (jnp.arange(FBLOCKS, dtype=jnp.int32) // FB % N_SOLID).astype(jnp.int32)
    target = ((block_owner[:, 0] * N_SOLID + home) * SR + block_row[:, 0]).astype(jnp.int32)
    force = jax.ops.segment_sum(mapped, target, NSR)
    solved = displacement
    denom = 4.0 + stiffness[:, None, :]
    for sweep in range(SWEEPS):
        rows = jnp.pad(solved, ((1, 1), (0, 0), (0, 0)))
        across = jnp.pad(solved, ((0, 0), (0, 0), (1, 1)))
        beside = rows[2:] + rows[:-2] + across[:, :, 2:] + across[:, :, :-2]
        solved = (force + beside) / denom
    residual = solved - displacement
    flat_res = residual_history.reshape(HIST, -1)
    flat = residual.reshape(-1)
    gram = jnp.dot(flat_res, flat_res.T, precision=lax.Precision.HIGHEST)
    proj = jnp.dot(flat_res, flat, precision=lax.Precision.HIGHEST)
    squares = jnp.sum(flat * flat)
    lower = jnp.linalg.cholesky(gram)
    coeff = jax.scipy.linalg.cho_solve((lower, True), -proj)
    update = jnp.dot(coeff, solution_history.reshape(HIST, -1), precision=lax.Precision.HIGHEST).reshape(solved.shape)
    next_displacement = solved + update
    shell = next_displacement.astype(jnp.bfloat16)
    picked = shell[target].astype(jnp.float32)
    wall_next = jnp.einsum('bpq,bcq->cbp', rbf, picked).reshape(3, NS)
    return (new_flow, next_displacement, wall_next, jnp.sqrt(squares))
```

```python
import jax
import jax.numpy as jnp
from jax import lax
from jax.experimental import pallas as pl
from jax.experimental.pallas import tpu as pltpu
from jax.sharding import PartitionSpec as P

MESH = pl.DeviceIdType.MESH
F32 = jnp.float32
BF16 = jnp.bfloat16
SWEEPS = 4
NF = 32
NS = 4
ND = NF * NS
BLOCKS = 64
BLK = 128
POINTS = BLOCKS * BLK
EDGE = 16
CHUNKS = 8
ROWS = 32
HIST = 64
ENT = 96
SLOTS = 16


def iota(shape, dim):
    return lax.broadcasted_iota(jnp.int32, shape, dim)


def dot(a, b):
    return jnp.dot(a, b, preferred_element_type=F32)


def dot_t(a, b):
    return lax.dot_general(a, b, (((1,), (1,)), ((), ())), preferred_element_type=F32)


def halves(x):
    hi = x.astype(BF16)
    return hi, (x - hi.astype(F32)).astype(BF16)


def kernel(
    flow, wm, aop, wc, ws, rbf, owner, row, disp, stiff, vh, wh,
    nf, nd, local, norm, rbv,
    fbuf, wmv, av, wcv, wsv, ownv, rowv, dbuf, sbuf, vv, wv,
    mapped, oh, oht, lab, gsend, gin1, gsum1, gin2, out, arrived, pt, fext,
    psend, pin1, psum1, pin2, cbuf, rep, back, resid, wide32, tract,
    lsem, ssem, rsem,
):
    f, s = lax.axis_index("fluid"), lax.axis_index("solid")
    me = f * NS + s
    nxt, prv = lax.rem(me + 1, ND), lax.rem(me + ND - 1, ND)
    nxt_id, prv_id = (nxt // NS, lax.rem(nxt, NS)), (prv // NS, lax.rem(prv, NS))
    core, chip = lax.rem(f, 2), f // 2
    near = core * NS + s

    def near_id(d):
        other = lax.rem(near + d, 8)
        return other, (chip * 2 + other // NS, lax.rem(other, NS))

    def far_id(d):
        other = lax.rem(chip + d, 16)
        return other, (other * 2 + core, s)

    barrier = pltpu.get_barrier_semaphore()

    def signal(device):
        pl.semaphore_signal(barrier, inc=1, device_id=device, device_id_type=MESH)

    def greet_fluid(d, carry):
        signal((lax.rem(f + d, NF), s))
        return carry

    lax.fori_loop(1, NF, greet_fluid, 0)

    def greet_near(d, carry):
        signal(near_id(d)[1])
        return carry

    lax.fori_loop(1, 8, greet_near, 0)
    signal(nxt_id)
    signal(prv_id)

    def load(src, dst, i):
        copy = pltpu.make_async_copy(src, dst, lsem.at[i])
        copy.start()
        return copy

    part = POINTS // CHUNKS
    l_own = load(owner, ownv, 0)
    l_row = load(row, rowv, 1)
    l_v = load(vh, vv, 2)
    l_a = load(aop, av, 3)
    l_wc = load(wc, wcv, 4)
    l_ws = load(ws, wsv, 5)
    l_wm = load(wm, wmv, 6)
    l_disp = load(disp, dbuf.at[:, pl.ds(8, ROWS), :], 7)
    l_stiff = load(stiff, sbuf.at[pl.ds(8, ROWS), :], 8)
    l_flow = [
        load(flow.at[:, pl.ds(i * part, part), :], fbuf.at[:, pl.ds(EDGE + i * part, part), :], 9 + i)
        for i in range(CHUNKS)
    ]
    l_rbf = load(rbf, rbv, 9 + CHUNKS)
    l_w = load(wh, wv, 10 + CHUNKS)

    l_own.wait()
    l_row.wait()
    own_row = ownv[...].astype(F32)
    lab_row = rowv[...].astype(F32)
    eye = iota((HIST, HIST), 0) == iota((HIST, HIST), 1)
    ones = jnp.ones((BLOCKS, 128), BF16)
    own_col = dot(jnp.where(eye, own_row, 0.0).astype(BF16), ones)
    lab[...] = dot(jnp.where(eye, lab_row, 0.0).astype(BF16), ones) + 1.0
    same = own_col[:, :BLOCKS] == own_row
    above = iota((BLOCKS, BLOCKS), 0) < iota((BLOCKS, BLOCKS), 1)
    before_row = jnp.sum(jnp.where(same & above, 1.0, 0.0), axis=0, keepdims=True)
    below = iota((BLOCKS, BLOCKS), 1) < iota((BLOCKS, BLOCKS), 0)
    before_col = dot(jnp.where(same & below, 1.0, 0.0).astype(BF16), ones)
    both = jnp.where(iota((16, BLOCKS), 0) == 0, own_row, before_row).astype(BF16)
    wide = dot(both, jnp.where(iota((BLOCKS, 512), 1) // 8 == iota((BLOCKS, 512), 0), 1.0, 0.0).astype(BF16))

    def target(own, before, comp):
        return own * SLOTS + jnp.where(comp < 3.0, before * 3.0 + comp, jnp.where(comp == 3.0, 9.0 + before, -1e6))

    tgt_row = target(wide[0:1], wide[1:2], lax.rem(iota((1, 512), 1), 8).astype(F32))
    oh[...] = jnp.where(iota((512, 512), 0).astype(F32) == tgt_row, 1.0, 0.0).astype(BF16)
    tall = jnp.where(iota((512, BLOCKS), 0) // 8 == iota((512, BLOCKS), 1), 1.0, 0.0).astype(BF16)
    tgt_col = target(
        dot(tall, own_col.astype(BF16)),
        dot(tall, before_col.astype(BF16)),
        lax.rem(iota((512, 128), 0), 8).astype(F32),
    )
    for t in range(4):
        oht[:, t * 128 : (t + 1) * 128] = jnp.where(
            (iota((512, 128), 1) + t * 128).astype(F32) == tgt_col, 1.0, 0.0
        ).astype(BF16)

    l_v.wait()

    def history(i):
        return vv[pl.ds(i, HIST, stride=ENT), :]

    def gram_step(t, acc):
        for u in range(4):
            i = t * 8 + u * 2
            x = jnp.concatenate([history(i), history(i + 1)], axis=1)
            hi, lo = halves(x)
            acc = acc + dot_t(hi, jnp.concatenate([hi, lo], axis=0))
        return acc

    gram = lax.fori_loop(0, ENT // 8, gram_step, jnp.zeros((HIST, 128), F32))
    half = 0.5 * gram[:, :HIST] + gram[:, HIST:]
    packed = jnp.concatenate([half[:32], half[32:]], axis=1)
    gsend[...] = packed
    gin1[near] = packed

    pl.semaphore_wait(barrier, NF - 1 + 7 + 2)

    def send(src, dst, i, device):
        pltpu.make_async_remote_copy(
            src_ref=src, dst_ref=dst, send_sem=ssem.at[i], recv_sem=rsem.at[i],
            device_id=device, device_id_type=MESH,
        ).start()

    def taken(ref, sem):
        pltpu.make_async_copy(ref, ref, sem).wait()

    l_disp.wait()
    l_stiff.wait()
    send(flow.at[:, pl.ds(POINTS - EDGE, EDGE), :], fbuf.at[:, pl.ds(0, EDGE), :], 0, nxt_id)
    send(flow.at[:, pl.ds(0, EDGE), :], fbuf.at[:, pl.ds(EDGE + POINTS, EDGE), :], 1, prv_id)
    send(dbuf.at[:, pl.ds(ROWS, 8), :], dbuf.at[:, pl.ds(0, 8), :], 2, nxt_id)
    send(dbuf.at[:, pl.ds(8, 8), :], dbuf.at[:, pl.ds(ROWS + 8, 8), :], 3, prv_id)
    send(sbuf.at[pl.ds(ROWS, 8), :], sbuf.at[pl.ds(0, 8), :], 4, nxt_id)
    send(sbuf.at[pl.ds(8, 8), :], sbuf.at[pl.ds(ROWS + 8, 8), :], 5, prv_id)

    def reduce_near(src, dst, i):
        def step(d, carry):
            send(src, dst.at[near], i, near_id(d)[1])
            return carry

        lax.fori_loop(1, 8, step, 0)

    def reduce_far(src, dst, i):
        def step(d, carry):
            send(src, dst.at[chip], i, far_id(d)[1])
            return carry

        lax.fori_loop(1, 16, step, 0)

    reduce_near(gsend, gin1, 6)

    l_a.wait()
    l_wc.wait()
    l_ws.wait()
    l_wm.wait()
    l_rbf.wait()
    a = av[...]
    coupling = wcv[...]

    def slab(chunk):
        for u in range(8):
            base = pl.multiple_of((chunk * 8 + u) * BLK, BLK)
            for c in range(3):
                ext = fbuf[c, pl.ds(base, BLK + 2 * EDGE), :]
                e = wide32.at[u * 3 + c]
                e[...] = ext.astype(F32)
                near_by = e[pl.ds(EDGE - 1, BLK), :] + e[pl.ds(EDGE + 1, BLK), :]
                drift = dot(ext[EDGE : EDGE + BLK], a)
                motion = jnp.broadcast_to(wmv[c : c + 1, pl.ds(base, BLK)], (BLK, 128)).T
                new = 0.5 * e[pl.ds(EDGE, BLK), :] + 0.25 * near_by + drift + motion * coupling
                nf[c, pl.ds(base, BLK), :] = new.astype(BF16)

    def slab_step(i, carry):
        slab(i)
        return carry

    l_flow[0].wait()
    l_flow[1].wait()
    for i in range(1, CHUNKS - 1):
        if i == 4:
            taken(gin1.at[pl.ds(0, 7)], rsem.at[6])
            total = gin1[0]
            for g in range(1, 8):
                total = total + gin1[g]
            gsum1[...] = total
            gin2[chip] = total
            reduce_far(gsum1, gin2, 7)
        l_flow[i + 1].wait()
        lax.fori_loop(i, i + 1, slab_step, 0)
    taken(fbuf.at[:, pl.ds(0, EDGE), :], rsem.at[0])
    taken(fbuf.at[:, pl.ds(0, EDGE), :], rsem.at[1])

    @pl.when(me == 0)
    def _():
        fbuf[:, 0:EDGE, :] = jnp.zeros((3, EDGE, 128), BF16)

    @pl.when(me == ND - 1)
    def _():
        fbuf[:, EDGE + POINTS :, :] = jnp.zeros((3, EDGE, 128), BF16)

    def slab_edge(i, carry):
        slab(i * (CHUNKS - 1))
        return carry

    lax.fori_loop(0, 2, slab_edge, 0)

    stencil = jnp.concatenate([jnp.broadcast_to(wsv[...].astype(F32), (16, 128))] * 3, axis=1)
    stencil = jnp.where(iota((16, 384), 1) // 128 == iota((16, 384), 0), stencil, 0.0).astype(BF16)

    def pull(i, carry):
        base = pl.multiple_of(i * 16 * BLK, BLK)
        x = jnp.concatenate([nf[c, pl.ds(base, 16 * BLK), :] for c in range(3)], axis=1)
        t = dot_t(stencil, x).astype(BF16)
        for u in range(16):
            tract[i * 16 + u] = t[:, u * 128 : (u + 1) * 128]
        return carry

    lax.fori_loop(0, BLOCKS // 16, pull, 0)
    sub = iota((8, 128), 0)

    def spread_out(i, carry):
        for u in range(16):
            b = i * 16 + u
            m = dot(tract[b], rbv[b])[:8]
            m = jnp.where(sub < 3, m, jnp.where(sub == 3, lab[pl.ds(b, 1), :], 0.0))
            mapped[pl.ds(pl.multiple_of(b * 8, 8), 8), :] = m
        return carry

    lax.fori_loop(0, BLOCKS // 16, spread_out, 0)

    hi, lo = halves(mapped[...])
    out[...] = (dot(oh[...], hi) + dot(oh[...], lo)).reshape(NF, SLOTS, 128)

    def exchange(src, dst, i):
        def step(d, carry):
            other = lax.rem(f + d, NF)
            send(src.at[other], dst.at[f], i, (other, s))
            return carry

        lax.fori_loop(1, NF, step, 0)
        pltpu.make_async_copy(src.at[f], dst.at[f], rsem.at[i]).start()

    exchange(out, arrived, 8)

    taken(gin2.at[pl.ds(0, 15)], rsem.at[7])
    total = gin2[0]
    for g in range(1, 16):
        total = total + gin2[g]
    half = jnp.concatenate([total[:, :HIST], total[:, HIST:]], axis=0)
    work = jnp.concatenate([half + half.T, jnp.where(eye, 1.0, 0.0)], axis=1)
    sub64 = iota((HIST, 128), 0)

    def eliminate(work, first, last):
        for k in range(first, last):
            pivot = work[k : k + 1, :] * (1.0 / work[k : k + 1, k : k + 1])
            work = jnp.where(sub64 == k, pivot, work - work[:, k : k + 1] * pivot)
        return work

    work = eliminate(work, 0, 24)

    taken(arrived, rsem.at[8])
    got = arrived[...]
    slot = iota((NF, SLOTS, 128), 1)
    label = jnp.where(slot < 3, got[:, 9:10], jnp.where(slot < 6, got[:, 10:11], got[:, 11:12]))
    lane = iota((NF, SLOTS, 128), 2)
    hit = (label == (lax.rem(lane, ROWS) + 1).astype(F32)) & (lane // ROWS == lax.rem(slot, 3)) & (slot < 9)
    pt[...] = jnp.where(hit, 1.0, 0.0).astype(BF16).reshape(512, 128)
    hi, lo = halves(got.reshape(512, 128))
    place = pt[...]

    def placed(x):
        return lax.dot_general(place, x, (((0,), (0,)), ((), ())), preferred_element_type=F32)

    force = placed(hi) + placed(lo)
    fext[:, pl.ds(8, ROWS), :] = force[:ENT].reshape(3, ROWS, 128)
    send(fext.at[:, pl.ds(ROWS, 8), :], fext.at[:, pl.ds(0, 8), :], 9, nxt_id)
    send(fext.at[:, pl.ds(8, 8), :], fext.at[:, pl.ds(ROWS + 8, 8), :], 10, prv_id)

    work = eliminate(work, 24, 40)

    for i in (2, 3):
        taken(dbuf.at[:, pl.ds(0, 8), :], rsem.at[i])
    for i in (4, 5):
        taken(sbuf.at[pl.ds(0, 8), :], rsem.at[i])
    for i in (9, 10):
        taken(fext.at[:, pl.ds(0, 8), :], rsem.at[i])

    long = ROWS + 16
    at_row = iota((3, long, 128), 1) + me * ROWS - 8
    inside = (at_row >= 0) & (at_row < ND * ROWS)
    inverse = jnp.where(inside, 1.0 / (4.0 + sbuf[...])[None], 0.0)
    loads = jnp.where(inside, fext[...], 0.0)
    solved = jnp.where(inside, dbuf[...], 0.0)
    start = solved[:, 8 : 8 + ROWS]
    q = iota((3, long, 128), 2)
    for _ in range(SWEEPS):
        zero = jnp.zeros((3, 1, 128), F32)
        up = jnp.concatenate([zero, solved[:, : long - 1]], axis=1)
        down = jnp.concatenate([solved[:, 1:], zero], axis=1)
        left = jnp.where(q == 0, 0.0, pltpu.roll(solved, 1, 2))
        right = jnp.where(q == 127, 0.0, pltpu.roll(solved, 127, 2))
        solved = (loads + ((up + down) + (left + right))) * inverse
    solved = solved[:, 8 : 8 + ROWS]
    residual = (solved - start).reshape(ENT, 128)
    solved = solved.reshape(ENT, 128)

    resid[...] = residual

    def project(t, acc):
        for c in range(3):
            r8 = resid[pl.ds(pl.multiple_of(c * ROWS + t * 8, 8), 8), :]
            for u in range(8):
                acc = acc + history(c * ROWS + t * 8 + u) * r8[u : u + 1]
        return acc

    proj = lax.fori_loop(0, ROWS // 8, project, jnp.zeros((HIST, 128), F32))
    square = jnp.sum((residual * residual).reshape(ENT // 8, 8, 128), axis=0)
    sums = jnp.concatenate([proj, square, jnp.zeros((128 - HIST - 8, 128), F32)], axis=0)
    hi = sums.astype(BF16)
    rest = sums - hi.astype(F32)
    mid, low = halves(rest)
    one8 = jnp.ones((16, 128), BF16)
    line = (dot_t(one8, hi) + dot_t(one8, mid) + dot_t(one8, low))[:8]
    psend[...] = line
    pin1[near] = line
    reduce_near(psend, pin1, 11)

    work = eliminate(work, 40, 52)

    taken(pin1.at[pl.ds(0, 7)], rsem.at[11])
    total = pin1[0]
    for g in range(1, 8):
        total = total + pin1[g]
    psum1[...] = total
    pin2[chip] = total
    reduce_far(psum1, pin2, 12)

    work = eliminate(work, 52, 64)
    l_w.wait()

    taken(pin2.at[pl.ds(0, 15)], rsem.at[12])
    total = pin2[0]
    for g in range(1, 16):
        total = total + pin2[g]
    weights = -jnp.sum(work[:, HIST:] * total[0:1, :HIST], axis=1, keepdims=True)
    cbuf[...] = jnp.broadcast_to(weights, (HIST, 128))
    lane8 = iota((8, 128), 1)
    squares = jnp.sum(jnp.where((lane8 >= HIST) & (lane8 < HIST + 8), total, 0.0), axis=1, keepdims=True)
    norm[...] = jnp.sqrt(squares[0:1])

    def update(t, acc):
        for u in range(8):
            j = t * 8 + u
            acc = acc + cbuf[pl.ds(j, 1), :] * wv[pl.ds(pl.multiple_of(j * ENT, 8), ENT), :]
        return acc

    moved = solved + lax.fori_loop(0, HIST // 8, update, jnp.zeros((ENT, 128), F32))
    nd[...] = moved

    shell = jnp.concatenate([moved, jnp.zeros((128 - ENT, 128), F32)], axis=0).astype(BF16)
    rep[...] = dot(pt[...], shell).astype(BF16).reshape(NF, SLOTS, 128)
    exchange(rep, back, 13)
    taken(back, rsem.at[13])
    local[...] = dot(oht[...], back[...].reshape(512, 128)).astype(BF16)

    for i, ref in (
        (0, fbuf.at[:, pl.ds(0, EDGE), :]), (1, fbuf.at[:, pl.ds(0, EDGE), :]),
        (2, dbuf.at[:, pl.ds(0, 8), :]), (3, dbuf.at[:, pl.ds(0, 8), :]),
        (4, sbuf.at[pl.ds(0, 8), :]), (5, sbuf.at[pl.ds(0, 8), :]),
        (6, gin1.at[pl.ds(0, 7)]), (7, gin2.at[pl.ds(0, 15)]),
        (8, arrived.at[pl.ds(0, NF - 1)]),
        (9, fext.at[:, pl.ds(0, 8), :]), (10, fext.at[:, pl.ds(0, 8), :]),
        (11, pin1.at[pl.ds(0, 7)]), (12, pin2.at[pl.ds(0, 15)]),
        (13, back.at[pl.ds(0, NF - 1)]),
    ):
        taken(ref, ssem.at[i])


def finish(nf, nd, local, norm, rbv, nf_out, nd_out, wn, norm_out, sems):
    copies = []
    for k in range(3):
        copies.append(pltpu.make_async_copy(nf.at[k], nf_out.at[k], sems.at[k]))
    copies.append(pltpu.make_async_copy(nd, nd_out, sems.at[3]))
    copies.append(pltpu.make_async_copy(norm, norm_out, sems.at[4]))
    for copy in copies:
        copy.start()

    def wall(i, carry):
        for u in range(16):
            b = i * 16 + u
            rows = local[pl.ds(pl.multiple_of(b * 8, 8), 8), :]
            wn[:, pl.ds(pl.multiple_of(b * BLK, BLK), BLK)] = dot_t(rows, rbv[b])[:3]
        return carry

    lax.fori_loop(0, BLOCKS // 16, wall, 0)
    for copy in copies:
        copy.wait()


def per_device(flow, wm, aop, wc, ws, rbf, owner, row, disp, stiff, vh, wh):
    any_ = pl.BlockSpec(memory_space=pl.ANY)
    vmem = pl.BlockSpec(memory_space=pltpu.VMEM)
    out = pl.pallas_call(
        kernel,
        name="coupling",
        out_shape=(
            pltpu.VMEM((3, POINTS, 128), BF16),
            pltpu.VMEM((ENT, 128), F32),
            pltpu.VMEM((BLOCKS * 8, 128), BF16),
            pltpu.VMEM((1, 1), F32),
            pltpu.VMEM((BLOCKS, BLK, 128), BF16),
        ),
        in_specs=[pl.BlockSpec(memory_space=pltpu.HBM)] * 12,
        out_specs=(vmem,) * 5,
        scratch_shapes=[
            pltpu.VMEM((3, POINTS + 2 * EDGE, 128), BF16),
            pltpu.VMEM((3, POINTS), F32),
            pltpu.VMEM((128, 128), BF16),
            pltpu.VMEM((1, 128), F32),
            pltpu.VMEM((1, 128), BF16),
            pltpu.VMEM((1, BLOCKS), jnp.int32),
            pltpu.VMEM((1, BLOCKS), jnp.int32),
            pltpu.VMEM((3, ROWS + 16, 128), F32),
            pltpu.VMEM((ROWS + 16, 128), F32),
            pltpu.VMEM((HIST * ENT, 128), F32),
            pltpu.VMEM((HIST * ENT, 128), F32),
            pltpu.VMEM((BLOCKS * 8, 128), F32),
            pltpu.VMEM((512, 512), BF16),
            pltpu.VMEM((512, 512), BF16),
            pltpu.VMEM((BLOCKS, 128), F32),
            pltpu.VMEM((32, 128), F32),
            pltpu.VMEM((8, 32, 128), F32),
            pltpu.VMEM((32, 128), F32),
            pltpu.VMEM((16, 32, 128), F32),
            pltpu.VMEM((NF, SLOTS, 128), F32),
            pltpu.VMEM((NF, SLOTS, 128), F32),
            pltpu.VMEM((512, 128), BF16),
            pltpu.VMEM((3, ROWS + 16, 128), F32),
            pltpu.VMEM((8, 128), F32),
            pltpu.VMEM((8, 8, 128), F32),
            pltpu.VMEM((8, 128), F32),
            pltpu.VMEM((16, 8, 128), F32),
            pltpu.VMEM((HIST, 128), F32),
            pltpu.VMEM((NF, SLOTS, 128), BF16),
            pltpu.VMEM((NF, SLOTS, 128), BF16),
            pltpu.VMEM((ENT, 128), F32),
            pltpu.VMEM((24, BLK + 2 * EDGE, 128), F32),
            pltpu.VMEM((BLOCKS, 16, 128), BF16),
            pltpu.SemaphoreType.DMA((11 + CHUNKS,)),
            pltpu.SemaphoreType.DMA((14,)),
            pltpu.SemaphoreType.DMA((14,)),
        ],
        compiler_params=pltpu.CompilerParams(
            collective_id=0, has_side_effects=True, vmem_limit_bytes=55 << 20
        ),
    )(
        flow, wm, aop, wc.reshape(1, 128), ws.reshape(1, 128), rbf,
        owner.reshape(1, BLOCKS), row.reshape(1, BLOCKS),
        jnp.transpose(disp, (1, 0, 2)), stiff,
        jnp.transpose(vh, (0, 2, 1, 3)).reshape(HIST * ENT, 128),
        jnp.transpose(wh, (0, 2, 1, 3)).reshape(HIST * ENT, 128),
    )
    new_flow, moved, wall_next, norm = pl.pallas_call(
        finish,
        name="wall",
        out_shape=(
            jax.ShapeDtypeStruct((3, POINTS, 128), BF16),
            jax.ShapeDtypeStruct((ENT, 128), F32),
            jax.ShapeDtypeStruct((3, POINTS), F32),
            jax.ShapeDtypeStruct((1, 1), F32),
        ),
        in_specs=[vmem] * 5,
        out_specs=(any_, any_, vmem, any_),
        scratch_shapes=[pltpu.SemaphoreType.DMA((5,))],
        compiler_params=pltpu.CompilerParams(vmem_limit_bytes=8 << 20),
    )(*out)
    moved = jnp.transpose(moved.reshape(3, ROWS, 128), (1, 0, 2))
    return new_flow, moved, wall_next, norm.reshape(())


def solution(mesh):
    both = ("fluid", "solid")
    return jax.shard_map(
        per_device,
        mesh=mesh,
        in_specs=(
            P(None, both, None), P(None, both), P(), P(), P(), P(both, None, None), P(both, None), P(both, None),
            P(both, None, None), P(both, None), P(None, both, None, None), P(None, both, None, None),
        ),
        out_specs=(P(None, both, None), P(both, None, None), P(None, both), P()),
        check_vma=False,
    )
```

```python
import jax
import jax.numpy as jnp
from jax import lax
from jax.experimental import pallas as pl
from jax.experimental.pallas import tpu as pltpu
from jax.sharding import PartitionSpec as P

MESH = pl.DeviceIdType.MESH
F32 = jnp.float32
BF16 = jnp.bfloat16
SWEEPS = 4
NF = 32
NS = 4
ND = NF * NS
BLOCKS = 64
BLK = 128
POINTS = BLOCKS * BLK
EDGE = 16
CHUNKS = 8
ROWS = 32
HIST = 64
ENT = 96
SLOTS = 16


def iota(shape, dim):
    return lax.broadcasted_iota(jnp.int32, shape, dim)


def dot(a, b):
    return jnp.dot(a, b, preferred_element_type=F32)


def dot_t(a, b):
    return lax.dot_general(a, b, (((1,), (1,)), ((), ())), preferred_element_type=F32)


def halves(x):
    hi = x.astype(BF16)
    return hi, (x - hi.astype(F32)).astype(BF16)


def kernel(
    flow, wm, aop, wc, ws, rbf, owner, row, disp, stiff, vh, wh,
    nf, nd, local, norm, rbv,
    fbuf, wmv, av, wcv, wsv, ownv, rowv, dbuf, sbuf, vv, wv,
    mapped, oh, oht, lab, gsend, gin1, gsum1, gin2, out, arrived, pt, fext,
    psend, pin, cbuf, rep, back, resid, wide32, tract,
    lsem, ssem, rsem,
):
    f, s = lax.axis_index("fluid"), lax.axis_index("solid")
    me = f * NS + s
    nxt, prv = lax.rem(me + 1, ND), lax.rem(me + ND - 1, ND)
    nxt_id, prv_id = (nxt // NS, lax.rem(nxt, NS)), (prv // NS, lax.rem(prv, NS))
    core, chip = lax.rem(f, 2), f // 2
    near = core * NS + s

    def near_id(d):
        other = lax.rem(near + d, 8)
        return other, (chip * 2 + other // NS, lax.rem(other, NS))

    def far_id(d):
        other = lax.rem(chip + d, 16)
        return other, (other * 2 + core, s)

    barrier = pltpu.get_barrier_semaphore()

    def signal(device):
        pl.semaphore_signal(barrier, inc=1, device_id=device, device_id_type=MESH)

    def greet_fluid(d, carry):
        signal((lax.rem(f + d, NF), s))
        return carry

    lax.fori_loop(1, NF, greet_fluid, 0)

    def greet_near(d, carry):
        signal(near_id(d)[1])
        return carry

    lax.fori_loop(1, 8, greet_near, 0)
    signal(nxt_id)
    signal(prv_id)

    def load(src, dst, i):
        copy = pltpu.make_async_copy(src, dst, lsem.at[i])
        copy.start()
        return copy

    part = POINTS // CHUNKS
    l_own = load(owner, ownv, 0)
    l_row = load(row, rowv, 1)
    l_v = load(vh, vv, 2)
    l_a = load(aop, av, 3)
    l_wc = load(wc, wcv, 4)
    l_ws = load(ws, wsv, 5)
    l_wm = load(wm, wmv, 6)
    l_disp = load(disp, dbuf.at[:, pl.ds(8, ROWS), :], 7)
    l_stiff = load(stiff, sbuf.at[pl.ds(8, ROWS), :], 8)
    l_flow = [
        load(flow.at[:, pl.ds(i * part, part), :], fbuf.at[:, pl.ds(EDGE + i * part, part), :], 9 + i)
        for i in range(CHUNKS)
    ]
    l_rbf = load(rbf, rbv, 9 + CHUNKS)
    l_w = load(wh, wv, 10 + CHUNKS)

    l_own.wait()
    l_row.wait()
    own_row = ownv[...].astype(F32)
    lab_row = rowv[...].astype(F32)
    eye = iota((HIST, HIST), 0) == iota((HIST, HIST), 1)
    ones = jnp.ones((BLOCKS, 128), BF16)
    own_col = dot(jnp.where(eye, own_row, 0.0).astype(BF16), ones)
    lab[...] = dot(jnp.where(eye, lab_row, 0.0).astype(BF16), ones) + 1.0
    same = own_col[:, :BLOCKS] == own_row
    above = iota((BLOCKS, BLOCKS), 0) < iota((BLOCKS, BLOCKS), 1)
    before_row = jnp.sum(jnp.where(same & above, 1.0, 0.0), axis=0, keepdims=True)
    below = iota((BLOCKS, BLOCKS), 1) < iota((BLOCKS, BLOCKS), 0)
    before_col = dot(jnp.where(same & below, 1.0, 0.0).astype(BF16), ones)
    both = jnp.where(iota((16, BLOCKS), 0) == 0, own_row, before_row).astype(BF16)
    wide = dot(both, jnp.where(iota((BLOCKS, 512), 1) // 8 == iota((BLOCKS, 512), 0), 1.0, 0.0).astype(BF16))

    def target(own, before, comp):
        return own * SLOTS + jnp.where(comp < 3.0, before * 3.0 + comp, jnp.where(comp == 3.0, 9.0 + before, -1e6))

    tgt_row = target(wide[0:1], wide[1:2], lax.rem(iota((1, 512), 1), 8).astype(F32))
    oh[...] = jnp.where(iota((512, 512), 0).astype(F32) == tgt_row, 1.0, 0.0).astype(BF16)
    tall = jnp.where(iota((512, BLOCKS), 0) // 8 == iota((512, BLOCKS), 1), 1.0, 0.0).astype(BF16)
    tgt_col = target(
        dot(tall, own_col.astype(BF16)),
        dot(tall, before_col.astype(BF16)),
        lax.rem(iota((512, 128), 0), 8).astype(F32),
    )
    for t in range(4):
        oht[:, t * 128 : (t + 1) * 128] = jnp.where(
            (iota((512, 128), 1) + t * 128).astype(F32) == tgt_col, 1.0, 0.0
        ).astype(BF16)

    l_v.wait()

    def history(i):
        return vv[pl.ds(i, HIST, stride=ENT), :]

    def gram_step(t, acc):
        for u in range(4):
            i = t * 8 + u * 2
            x = jnp.concatenate([history(i), history(i + 1)], axis=1)
            hi, lo = halves(x)
            acc = acc + dot_t(hi, jnp.concatenate([hi, lo], axis=0))
        return acc

    gram = lax.fori_loop(0, ENT // 8, gram_step, jnp.zeros((HIST, 128), F32))
    half = 0.5 * gram[:, :HIST] + gram[:, HIST:]
    packed = jnp.concatenate([half[:32], half[32:]], axis=1)
    gsend[...] = packed
    gin1[near] = packed

    pl.semaphore_wait(barrier, NF - 1 + 7 + 2)

    def send(src, dst, i, device):
        pltpu.make_async_remote_copy(
            src_ref=src, dst_ref=dst, send_sem=ssem.at[i], recv_sem=rsem.at[i],
            device_id=device, device_id_type=MESH,
        ).start()

    def taken(ref, sem):
        pltpu.make_async_copy(ref, ref, sem).wait()

    l_disp.wait()
    l_stiff.wait()
    send(flow.at[:, pl.ds(POINTS - EDGE, EDGE), :], fbuf.at[:, pl.ds(0, EDGE), :], 0, nxt_id)
    send(flow.at[:, pl.ds(0, EDGE), :], fbuf.at[:, pl.ds(EDGE + POINTS, EDGE), :], 1, prv_id)
    send(dbuf.at[:, pl.ds(ROWS, 8), :], dbuf.at[:, pl.ds(0, 8), :], 2, nxt_id)
    send(dbuf.at[:, pl.ds(8, 8), :], dbuf.at[:, pl.ds(ROWS + 8, 8), :], 3, prv_id)
    send(sbuf.at[pl.ds(ROWS, 8), :], sbuf.at[pl.ds(0, 8), :], 4, nxt_id)
    send(sbuf.at[pl.ds(8, 8), :], sbuf.at[pl.ds(ROWS + 8, 8), :], 5, prv_id)

    def reduce_near(src, dst, i):
        def step(d, carry):
            send(src, dst.at[near], i, near_id(d)[1])
            return carry

        lax.fori_loop(1, 8, step, 0)

    def reduce_far(src, dst, i):
        def step(d, carry):
            send(src, dst.at[chip], i, far_id(d)[1])
            return carry

        lax.fori_loop(1, 16, step, 0)

    reduce_near(gsend, gin1, 6)

    l_a.wait()
    l_wc.wait()
    l_ws.wait()
    l_wm.wait()
    a = av[...]
    coupling = wcv[...]

    stencil = jnp.concatenate([jnp.broadcast_to(wsv[...].astype(F32), (16, 128))] * 3, axis=1)
    stencil = jnp.where(iota((16, 384), 1) // 128 == iota((16, 384), 0), stencil, 0.0).astype(BF16)
    sub = iota((8, 128), 0)

    def slab(b, u):
        base = pl.multiple_of(b * BLK, BLK)
        for c in range(3):
            ext = fbuf[c, pl.ds(base, BLK + 2 * EDGE), :]
            e = wide32.at[u * 3 + c]
            e[...] = ext.astype(F32)
            near_by = e[pl.ds(EDGE - 1, BLK), :] + e[pl.ds(EDGE + 1, BLK), :]
            drift = dot(ext[EDGE : EDGE + BLK], a)
            motion = jnp.broadcast_to(wmv[c : c + 1, pl.ds(base, BLK)], (BLK, 128)).T
            new = 0.5 * e[pl.ds(EDGE, BLK), :] + 0.25 * near_by + drift + motion * coupling
            nf[c, pl.ds(base, BLK), :] = new.astype(BF16)

    def slab_step(i, carry):
        for u in range(8):
            slab(i * 8 + u, u)
        return carry

    def pull(points):
        x = jnp.concatenate([nf[c, points, :] for c in range(3)], axis=1)
        return dot_t(stencil, x).astype(BF16)

    def spread_out(b, tractions):
        m = dot(tractions, rbv[b])[:8]
        m = jnp.where(sub < 3, m, jnp.where(sub == 3, lab[pl.ds(b, 1), :], 0.0))
        mapped[pl.ds(pl.multiple_of(b * 8, 8), 8), :] = m

    def pull_step(i, carry):
        t = pull(pl.ds(pl.multiple_of(i * 16 * BLK, BLK), 16 * BLK))
        for u in range(16):
            tract[i * 16 + u] = t[:, u * 128 : (u + 1) * 128]
        return carry

    def map_step(i, carry):
        for u in range(16):
            spread_out(i * 16 + u, tract[i * 16 + u])
        return carry

    ends = (0, BLOCKS - 1)
    for b in ends:
        nf[:, b * BLK : (b + 1) * BLK, :] = jnp.zeros((3, BLK, 128), BF16)
    l_flow[0].wait()
    l_flow[1].wait()
    for u in range(1, 8):
        slab(u, u)
    for i in range(1, CHUNKS - 1):
        l_flow[i + 1].wait()
        lax.fori_loop(i, i + 1, slab_step, 0)
    for u in range(7):
        slab(BLOCKS - 8 + u, u)
    l_rbf.wait()
    lax.fori_loop(0, BLOCKS // 16, pull_step, 0)
    lax.fori_loop(0, BLOCKS // 16, map_step, 0)

    taken(gin1.at[pl.ds(0, 7)], rsem.at[6])
    total = gin1[0]
    for g in range(1, 8):
        total = total + gin1[g]
    gsum1[...] = total
    gin2[chip] = total
    reduce_far(gsum1, gin2, 7)

    taken(fbuf.at[:, pl.ds(0, EDGE), :], rsem.at[0])
    taken(fbuf.at[:, pl.ds(0, EDGE), :], rsem.at[1])

    @pl.when(me == 0)
    def _():
        fbuf[:, 0:EDGE, :] = jnp.zeros((3, EDGE, 128), BF16)

    @pl.when(me == ND - 1)
    def _():
        fbuf[:, EDGE + POINTS :, :] = jnp.zeros((3, EDGE, 128), BF16)

    for u, b in enumerate(ends):
        slab(b, u)
    for b in ends:
        spread_out(b, pull(pl.ds(b * BLK, BLK)))

    hi, lo = halves(mapped[...])
    out[...] = (dot(oh[...], hi) + dot(oh[...], lo)).reshape(NF, SLOTS, 128)

    def exchange(src, dst, i):
        def step(d, carry):
            other = lax.rem(f + d, NF)
            send(src.at[other], dst.at[f], i, (other, s))
            return carry

        lax.fori_loop(1, NF, step, 0)
        pltpu.make_async_copy(src.at[f], dst.at[f], rsem.at[i]).start()

    exchange(out, arrived, 8)

    taken(arrived, rsem.at[8])
    got = arrived[...]
    slot = iota((NF, SLOTS, 128), 1)
    label = jnp.where(slot < 3, got[:, 9:10], jnp.where(slot < 6, got[:, 10:11], got[:, 11:12]))
    lane = iota((NF, SLOTS, 128), 2)
    hit = (label == (lax.rem(lane, ROWS) + 1).astype(F32)) & (lane // ROWS == lax.rem(slot, 3)) & (slot < 9)
    pt[...] = jnp.where(hit, 1.0, 0.0).astype(BF16).reshape(512, 128)
    hi, lo = halves(got.reshape(512, 128))
    place = pt[...]

    def placed(x):
        return lax.dot_general(place, x, (((0,), (0,)), ((), ())), preferred_element_type=F32)

    force = placed(hi) + placed(lo)
    fext[:, pl.ds(8, ROWS), :] = force[:ENT].reshape(3, ROWS, 128)
    send(fext.at[:, pl.ds(ROWS, 8), :], fext.at[:, pl.ds(0, 8), :], 9, nxt_id)
    send(fext.at[:, pl.ds(8, 8), :], fext.at[:, pl.ds(ROWS + 8, 8), :], 10, prv_id)

    taken(gin2.at[pl.ds(0, 15)], rsem.at[7])
    total = gin2[0]
    for g in range(1, 16):
        total = total + gin2[g]
    half = jnp.concatenate([total[:, :HIST], total[:, HIST:]], axis=0)
    work = jnp.concatenate([half + half.T, jnp.where(eye, 1.0, 0.0)], axis=1)
    sub64 = iota((HIST, 128), 0)

    def eliminate(work, first, last):
        for k in range(first, last):
            pivot = work[k : k + 1, :] * (1.0 / work[k : k + 1, k : k + 1])
            work = jnp.where(sub64 == k, pivot, work - work[:, k : k + 1] * pivot)
        return work

    work = eliminate(work, 0, 28)

    for i in (2, 3):
        taken(dbuf.at[:, pl.ds(0, 8), :], rsem.at[i])
    for i in (4, 5):
        taken(sbuf.at[pl.ds(0, 8), :], rsem.at[i])
    for i in (9, 10):
        taken(fext.at[:, pl.ds(0, 8), :], rsem.at[i])

    long = ROWS + 16
    at_row = iota((3, long, 128), 1) + me * ROWS - 8
    inside = (at_row >= 0) & (at_row < ND * ROWS)
    inverse = jnp.where(inside, 1.0 / (4.0 + sbuf[...])[None], 0.0)
    loads = jnp.where(inside, fext[...], 0.0)
    solved = jnp.where(inside, dbuf[...], 0.0)
    start = solved[:, 8 : 8 + ROWS]
    q = iota((3, long, 128), 2)
    for _ in range(SWEEPS):
        zero = jnp.zeros((3, 1, 128), F32)
        up = jnp.concatenate([zero, solved[:, : long - 1]], axis=1)
        down = jnp.concatenate([solved[:, 1:], zero], axis=1)
        left = jnp.where(q == 0, 0.0, pltpu.roll(solved, 1, 2))
        right = jnp.where(q == 127, 0.0, pltpu.roll(solved, 127, 2))
        solved = (loads + ((up + down) + (left + right))) * inverse
    solved = solved[:, 8 : 8 + ROWS]
    residual = (solved - start).reshape(ENT, 128)
    solved = solved.reshape(ENT, 128)

    resid[...] = residual

    def project(t, accs):
        accs = list(accs)
        for u in range(48):
            i = t * 48 + u
            accs[u % 4] = accs[u % 4] + history(i) * resid[pl.ds(i, 1), :]
        return tuple(accs)

    accs = lax.fori_loop(0, 2, project, (jnp.zeros((HIST, 128), F32),) * 4)
    proj = (accs[0] + accs[1]) + (accs[2] + accs[3])
    square = jnp.sum((residual * residual).reshape(ENT // 8, 8, 128), axis=0)
    sums = jnp.concatenate([proj, square, jnp.zeros((128 - HIST - 8, 128), F32)], axis=0)
    hi = sums.astype(BF16)
    rest = sums - hi.astype(F32)
    mid, low = halves(rest)
    one8 = jnp.ones((16, 128), BF16)
    line = (dot_t(one8, hi) + dot_t(one8, mid) + dot_t(one8, low))[:1]
    psend[...] = line
    pin[me] = line

    def tell(d, carry):
        other = lax.rem(me + d, ND)
        send(psend, pin.at[me], 11, (other // NS, lax.rem(other, NS)))
        return carry

    lax.fori_loop(1, ND, tell, 0)

    work = eliminate(work, 28, 64)
    l_w.wait()

    taken(pin.at[pl.ds(0, ND - 1)], rsem.at[11])
    total = jnp.sum(pin[...], axis=0)
    weights = -jnp.sum(work[:, HIST:] * total[0:1, :HIST], axis=1, keepdims=True)
    cbuf[...] = jnp.broadcast_to(weights, (HIST, 128))
    lane1 = iota((1, 128), 1)
    squares = jnp.sum(jnp.where((lane1 >= HIST) & (lane1 < HIST + 8), total, 0.0), axis=1, keepdims=True)
    norm[...] = jnp.sqrt(squares)

    def update(t, acc):
        for u in range(8):
            j = t * 8 + u
            acc = acc + cbuf[pl.ds(j, 1), :] * wv[pl.ds(pl.multiple_of(j * ENT, 8), ENT), :]
        return acc

    moved = solved + lax.fori_loop(0, HIST // 8, update, jnp.zeros((ENT, 128), F32))
    nd[...] = moved

    shell = jnp.concatenate([moved, jnp.zeros((128 - ENT, 128), F32)], axis=0).astype(BF16)
    rep[...] = dot(pt[...], shell).astype(BF16).reshape(NF, SLOTS, 128)
    exchange(rep, back, 12)
    taken(back, rsem.at[12])
    local[...] = dot(oht[...], back[...].reshape(512, 128)).astype(BF16)

    for i, ref in (
        (0, fbuf.at[:, pl.ds(0, EDGE), :]), (1, fbuf.at[:, pl.ds(0, EDGE), :]),
        (2, dbuf.at[:, pl.ds(0, 8), :]), (3, dbuf.at[:, pl.ds(0, 8), :]),
        (4, sbuf.at[pl.ds(0, 8), :]), (5, sbuf.at[pl.ds(0, 8), :]),
        (6, gin1.at[pl.ds(0, 7)]), (7, gin2.at[pl.ds(0, 15)]),
        (8, arrived.at[pl.ds(0, NF - 1)]),
        (9, fext.at[:, pl.ds(0, 8), :]), (10, fext.at[:, pl.ds(0, 8), :]),
        (11, pin.at[pl.ds(0, ND - 1)]),
        (12, back.at[pl.ds(0, NF - 1)]),
    ):
        taken(ref, ssem.at[i])


def finish(nf, nd, local, norm, rbv, nf_out, nd_out, wn, norm_out, sems):
    copies = []
    for k in range(3):
        copies.append(pltpu.make_async_copy(nf.at[k], nf_out.at[k], sems.at[k]))
    copies.append(pltpu.make_async_copy(nd, nd_out, sems.at[3]))
    copies.append(pltpu.make_async_copy(norm, norm_out, sems.at[4]))
    for copy in copies:
        copy.start()

    def wall(i, carry):
        for u in range(16):
            b = i * 16 + u
            rows = local[pl.ds(pl.multiple_of(b * 8, 8), 8), :]
            wn[:, pl.ds(pl.multiple_of(b * BLK, BLK), BLK)] = dot_t(rows, rbv[b])[:3]
        return carry

    lax.fori_loop(0, BLOCKS // 16, wall, 0)
    for copy in copies:
        copy.wait()


def per_device(flow, wm, aop, wc, ws, rbf, owner, row, disp, stiff, vh, wh):
    any_ = pl.BlockSpec(memory_space=pl.ANY)
    vmem = pl.BlockSpec(memory_space=pltpu.VMEM)
    out = pl.pallas_call(
        kernel,
        name="coupling",
        out_shape=(
            pltpu.VMEM((3, POINTS, 128), BF16),
            pltpu.VMEM((ENT, 128), F32),
            pltpu.VMEM((BLOCKS * 8, 128), BF16),
            pltpu.VMEM((1, 1), F32),
            pltpu.VMEM((BLOCKS, BLK, 128), BF16),
        ),
        in_specs=[pl.BlockSpec(memory_space=pltpu.HBM)] * 12,
        out_specs=(vmem,) * 5,
        scratch_shapes=[
            pltpu.VMEM((3, POINTS + 2 * EDGE, 128), BF16),
            pltpu.VMEM((3, POINTS), F32),
            pltpu.VMEM((128, 128), BF16),
            pltpu.VMEM((1, 128), F32),
            pltpu.VMEM((1, 128), BF16),
            pltpu.VMEM((1, BLOCKS), jnp.int32),
            pltpu.VMEM((1, BLOCKS), jnp.int32),
            pltpu.VMEM((3, ROWS + 16, 128), F32),
            pltpu.VMEM((ROWS + 16, 128), F32),
            pltpu.VMEM((HIST * ENT, 128), F32),
            pltpu.VMEM((HIST * ENT, 128), F32),
            pltpu.VMEM((BLOCKS * 8, 128), F32),
            pltpu.VMEM((512, 512), BF16),
            pltpu.VMEM((512, 512), BF16),
            pltpu.VMEM((BLOCKS, 128), F32),
            pltpu.VMEM((32, 128), F32),
            pltpu.VMEM((8, 32, 128), F32),
            pltpu.VMEM((32, 128), F32),
            pltpu.VMEM((16, 32, 128), F32),
            pltpu.VMEM((NF, SLOTS, 128), F32),
            pltpu.VMEM((NF, SLOTS, 128), F32),
            pltpu.VMEM((512, 128), BF16),
            pltpu.VMEM((3, ROWS + 16, 128), F32),
            pltpu.VMEM((1, 128), F32),
            pltpu.VMEM((ND, 1, 128), F32),
            pltpu.VMEM((HIST, 128), F32),
            pltpu.VMEM((NF, SLOTS, 128), BF16),
            pltpu.VMEM((NF, SLOTS, 128), BF16),
            pltpu.VMEM((ENT, 128), F32),
            pltpu.VMEM((24, BLK + 2 * EDGE, 128), F32),
            pltpu.VMEM((BLOCKS, 16, 128), BF16),
            pltpu.SemaphoreType.DMA((11 + CHUNKS,)),
            pltpu.SemaphoreType.DMA((13,)),
            pltpu.SemaphoreType.DMA((13,)),
        ],
        compiler_params=pltpu.CompilerParams(
            collective_id=0, has_side_effects=True, vmem_limit_bytes=55 << 20
        ),
    )(
        flow, wm, aop, wc.reshape(1, 128), ws.reshape(1, 128), rbf,
        owner.reshape(1, BLOCKS), row.reshape(1, BLOCKS),
        jnp.transpose(disp, (1, 0, 2)), stiff,
        jnp.transpose(vh, (0, 2, 1, 3)).reshape(HIST * ENT, 128),
        jnp.transpose(wh, (0, 2, 1, 3)).reshape(HIST * ENT, 128),
    )
    new_flow, moved, wall_next, norm = pl.pallas_call(
        finish,
        name="wall",
        out_shape=(
            jax.ShapeDtypeStruct((3, POINTS, 128), BF16),
            jax.ShapeDtypeStruct((ENT, 128), F32),
            jax.ShapeDtypeStruct((3, POINTS), F32),
            jax.ShapeDtypeStruct((1, 1), F32),
        ),
        in_specs=[vmem] * 5,
        out_specs=(any_, any_, vmem, any_),
        scratch_shapes=[pltpu.SemaphoreType.DMA((5,))],
        compiler_params=pltpu.CompilerParams(vmem_limit_bytes=8 << 20),
    )(*out)
    moved = jnp.transpose(moved.reshape(3, ROWS, 128), (1, 0, 2))
    return new_flow, moved, wall_next, norm.reshape(())


def solution(mesh):
    both = ("fluid", "solid")
    return jax.shard_map(
        per_device,
        mesh=mesh,
        in_specs=(
            P(None, both, None), P(None, both), P(), P(), P(), P(both, None, None), P(both, None), P(both, None),
            P(both, None, None), P(both, None), P(None, both, None, None), P(None, both, None, None),
        ),
        out_specs=(P(None, both, None), P(both, None, None), P(None, both), P()),
        check_vma=False,
    )
```

```python
import jax
import jax.numpy as jnp
from jax import lax
from jax.experimental import pallas as pl
from jax.experimental.pallas import tpu as pltpu
from jax.sharding import PartitionSpec as P

MESH = pl.DeviceIdType.MESH
F32 = jnp.float32
BF16 = jnp.bfloat16
SWEEPS = 4
NF = 32
NS = 4
ND = NF * NS
BLOCKS = 64
BLK = 128
POINTS = BLOCKS * BLK
EDGE = 16
CHUNKS = 8
ROWS = 32
HIST = 64
ENT = 96
SLOTS = 16


def iota(shape, dim):
    return lax.broadcasted_iota(jnp.int32, shape, dim)


def dot(a, b):
    return jnp.dot(a, b, preferred_element_type=F32)


def dot_t(a, b):
    return lax.dot_general(a, b, (((1,), (1,)), ((), ())), preferred_element_type=F32)


def halves(x):
    hi = x.astype(BF16)
    return hi, (x - hi.astype(F32)).astype(BF16)


def kernel(
    flow, wm, aop, wc, ws, rbf, owner, row, disp, stiff, vh, wh,
    nf, nd, local, norm, rbv,
    fbuf, wmv, av, wcv, wsv, ownv, rowv, dbuf, sbuf, vv, wv,
    mapped, oh, oht, lab, gsend, gin1, gsum1, gin2, out, arrived, pt, fext,
    psend, pin, cbuf, rep, back, resid, wide32, tract,
    lsem, ssem, rsem,
):
    f, s = lax.axis_index("fluid"), lax.axis_index("solid")
    me = f * NS + s
    nxt, prv = lax.rem(me + 1, ND), lax.rem(me + ND - 1, ND)
    nxt_id, prv_id = (nxt // NS, lax.rem(nxt, NS)), (prv // NS, lax.rem(prv, NS))
    core, chip = lax.rem(f, 2), f // 2
    near = core * NS + s

    def near_id(d):
        other = lax.rem(near + d, 8)
        return other, (chip * 2 + other // NS, lax.rem(other, NS))

    def far_id(d):
        other = lax.rem(chip + d, 16)
        return other, (other * 2 + core, s)

    barrier = pltpu.get_barrier_semaphore()

    def signal(device):
        pl.semaphore_signal(barrier, inc=1, device_id=device, device_id_type=MESH)

    def greet_fluid(d, carry):
        signal((lax.rem(f + d, NF), s))
        return carry

    lax.fori_loop(1, NF, greet_fluid, 0)

    def greet_near(d, carry):
        signal(near_id(d)[1])
        return carry

    lax.fori_loop(1, 8, greet_near, 0)
    signal(nxt_id)
    signal(prv_id)

    def load(src, dst, i):
        copy = pltpu.make_async_copy(src, dst, lsem.at[i])
        copy.start()
        return copy

    part = POINTS // CHUNKS
    l_a = load(aop, av, 3)
    l_wc = load(wc, wcv, 4)
    l_ws = load(ws, wsv, 5)
    l_wm = load(wm, wmv, 6)
    l_flow = [
        load(flow.at[:, pl.ds(i * part, part), :], fbuf.at[:, pl.ds(EDGE + i * part, part), :], 9 + i)
        for i in range(CHUNKS)
    ]
    l_own = load(owner, ownv, 0)
    l_row = load(row, rowv, 1)
    l_disp = load(disp, dbuf.at[:, pl.ds(8, ROWS), :], 7)
    l_stiff = load(stiff, sbuf.at[pl.ds(8, ROWS), :], 8)
    l_rbf = load(rbf, rbv, 9 + CHUNKS)
    l_v = load(vh, vv, 2)
    l_w = load(wh, wv, 10 + CHUNKS)

    def send(src, dst, i, device):
        pltpu.make_async_remote_copy(
            src_ref=src, dst_ref=dst, send_sem=ssem.at[i], recv_sem=rsem.at[i],
            device_id=device, device_id_type=MESH,
        ).start()

    def taken(ref, sem):
        pltpu.make_async_copy(ref, ref, sem).wait()

    def reduce_near(src, dst, i):
        def step(d, carry):
            send(src, dst.at[near], i, near_id(d)[1])
            return carry

        lax.fori_loop(1, 8, step, 0)

    def reduce_far(src, dst, i):
        def step(d, carry):
            send(src, dst.at[chip], i, far_id(d)[1])
            return carry

        lax.fori_loop(1, 16, step, 0)

    l_a.wait()
    l_wc.wait()
    l_ws.wait()
    l_wm.wait()
    a = av[...]
    coupling = wcv[...]

    stencil = jnp.concatenate([jnp.broadcast_to(wsv[...].astype(F32), (16, 128))] * 3, axis=1)
    stencil = jnp.where(iota((16, 384), 1) // 128 == iota((16, 384), 0), stencil, 0.0).astype(BF16)
    sub = iota((8, 128), 0)

    def slab(b, u):
        base = pl.multiple_of(b * BLK, BLK)
        for c in range(3):
            ext = fbuf[c, pl.ds(base, BLK + 2 * EDGE), :]
            e = wide32.at[u * 3 + c]
            e[...] = ext.astype(F32)
            near_by = e[pl.ds(EDGE - 1, BLK), :] + e[pl.ds(EDGE + 1, BLK), :]
            drift = dot(ext[EDGE : EDGE + BLK], a)
            motion = jnp.broadcast_to(wmv[c : c + 1, pl.ds(base, BLK)], (BLK, 128)).T
            new = 0.5 * e[pl.ds(EDGE, BLK), :] + 0.25 * near_by + drift + motion * coupling
            nf[c, pl.ds(base, BLK), :] = new.astype(BF16)

    def slab_step(i, carry):
        for u in range(8):
            slab(i * 8 + u, u)
        return carry

    def pull(points):
        x = jnp.concatenate([nf[c, points, :] for c in range(3)], axis=1)
        return dot_t(stencil, x).astype(BF16)

    def spread_out(b, tractions):
        m = dot(tractions, rbv[b])[:8]
        m = jnp.where(sub < 3, m, jnp.where(sub == 3, lab[pl.ds(b, 1), :], 0.0))
        mapped[pl.ds(pl.multiple_of(b * 8, 8), 8), :] = m

    def pull_step(i, carry):
        t = pull(pl.ds(pl.multiple_of(i * 16 * BLK, BLK), 16 * BLK))
        for u in range(16):
            tract[i * 16 + u] = t[:, u * 128 : (u + 1) * 128]
        return carry

    def map_step(i, carry):
        for u in range(16):
            spread_out(i * 16 + u, tract[i * 16 + u])
        return carry

    ends = (0, BLOCKS - 1)
    for b in ends:
        nf[:, b * BLK : (b + 1) * BLK, :] = jnp.zeros((3, BLK, 128), BF16)
    l_flow[0].wait()
    l_flow[1].wait()
    for u in range(1, 8):
        slab(u, u)
    for i in range(1, CHUNKS - 1):
        l_flow[i + 1].wait()
        lax.fori_loop(i, i + 1, slab_step, 0)
    for u in range(7):
        slab(BLOCKS - 8 + u, u)

    pl.semaphore_wait(barrier, NF - 1 + 7 + 2)

    l_disp.wait()
    l_stiff.wait()
    send(flow.at[:, pl.ds(POINTS - EDGE, EDGE), :], fbuf.at[:, pl.ds(0, EDGE), :], 0, nxt_id)
    send(flow.at[:, pl.ds(0, EDGE), :], fbuf.at[:, pl.ds(EDGE + POINTS, EDGE), :], 1, prv_id)
    send(dbuf.at[:, pl.ds(ROWS, 8), :], dbuf.at[:, pl.ds(0, 8), :], 2, nxt_id)
    send(dbuf.at[:, pl.ds(8, 8), :], dbuf.at[:, pl.ds(ROWS + 8, 8), :], 3, prv_id)
    send(sbuf.at[pl.ds(ROWS, 8), :], sbuf.at[pl.ds(0, 8), :], 4, nxt_id)
    send(sbuf.at[pl.ds(8, 8), :], sbuf.at[pl.ds(ROWS + 8, 8), :], 5, prv_id)

    lax.fori_loop(0, BLOCKS // 16, pull_step, 0)

    l_own.wait()
    l_row.wait()
    own_row = ownv[...].astype(F32)
    lab_row = rowv[...].astype(F32)
    eye = iota((HIST, HIST), 0) == iota((HIST, HIST), 1)
    ones = jnp.ones((BLOCKS, 128), BF16)
    own_col = dot(jnp.where(eye, own_row, 0.0).astype(BF16), ones)
    lab[...] = dot(jnp.where(eye, lab_row, 0.0).astype(BF16), ones) + 1.0
    same = own_col[:, :BLOCKS] == own_row
    above = iota((BLOCKS, BLOCKS), 0) < iota((BLOCKS, BLOCKS), 1)
    before_row = jnp.sum(jnp.where(same & above, 1.0, 0.0), axis=0, keepdims=True)
    below = iota((BLOCKS, BLOCKS), 1) < iota((BLOCKS, BLOCKS), 0)
    before_col = dot(jnp.where(same & below, 1.0, 0.0).astype(BF16), ones)
    both = jnp.where(iota((16, BLOCKS), 0) == 0, own_row, before_row).astype(BF16)
    wide = dot(both, jnp.where(iota((BLOCKS, 512), 1) // 8 == iota((BLOCKS, 512), 0), 1.0, 0.0).astype(BF16))

    def target(own, before, comp):
        return own * SLOTS + jnp.where(comp < 3.0, before * 3.0 + comp, jnp.where(comp == 3.0, 9.0 + before, -1e6))

    tgt_row = target(wide[0:1], wide[1:2], lax.rem(iota((1, 512), 1), 8).astype(F32))
    oh[...] = jnp.where(iota((512, 512), 0).astype(F32) == tgt_row, 1.0, 0.0).astype(BF16)
    tall = jnp.where(iota((512, BLOCKS), 0) // 8 == iota((512, BLOCKS), 1), 1.0, 0.0).astype(BF16)
    tgt_col = target(
        dot(tall, own_col.astype(BF16)),
        dot(tall, before_col.astype(BF16)),
        lax.rem(iota((512, 128), 0), 8).astype(F32),
    )
    for t in range(4):
        oht[:, t * 128 : (t + 1) * 128] = jnp.where(
            (iota((512, 128), 1) + t * 128).astype(F32) == tgt_col, 1.0, 0.0
        ).astype(BF16)

    l_rbf.wait()
    lax.fori_loop(0, BLOCKS // 16, map_step, 0)

    taken(fbuf.at[:, pl.ds(0, EDGE), :], rsem.at[0])
    taken(fbuf.at[:, pl.ds(0, EDGE), :], rsem.at[1])

    @pl.when(me == 0)
    def _():
        fbuf[:, 0:EDGE, :] = jnp.zeros((3, EDGE, 128), BF16)

    @pl.when(me == ND - 1)
    def _():
        fbuf[:, EDGE + POINTS :, :] = jnp.zeros((3, EDGE, 128), BF16)

    for u, b in enumerate(ends):
        slab(b, u)
    for b in ends:
        spread_out(b, pull(pl.ds(b * BLK, BLK)))

    hi, lo = halves(mapped[...])
    out[...] = (dot(oh[...], hi) + dot(oh[...], lo)).reshape(NF, SLOTS, 128)

    def exchange(src, dst, i):
        def step(d, carry):
            other = lax.rem(f + d, NF)
            send(src.at[other], dst.at[f], i, (other, s))
            return carry

        lax.fori_loop(1, NF, step, 0)
        pltpu.make_async_copy(src.at[f], dst.at[f], rsem.at[i]).start()

    exchange(out, arrived, 8)

    l_v.wait()

    def history(i):
        return vv[pl.ds(i, HIST, stride=ENT), :]

    def gram_step(t, acc):
        for u in range(4):
            i = t * 8 + u * 2
            x = jnp.concatenate([history(i), history(i + 1)], axis=1)
            hi, lo = halves(x)
            acc = acc + dot_t(hi, jnp.concatenate([hi, lo], axis=0))
        return acc

    gram = lax.fori_loop(0, ENT // 8, gram_step, jnp.zeros((HIST, 128), F32))
    half = 0.5 * gram[:, :HIST] + gram[:, HIST:]
    packed = jnp.concatenate([half[:32], half[32:]], axis=1)
    gsend[...] = packed
    gin1[near] = packed
    reduce_near(gsend, gin1, 6)

    taken(arrived, rsem.at[8])
    got = arrived[...]
    slot = iota((NF, SLOTS, 128), 1)
    label = jnp.where(slot < 3, got[:, 9:10], jnp.where(slot < 6, got[:, 10:11], got[:, 11:12]))
    lane = iota((NF, SLOTS, 128), 2)
    hit = (label == (lax.rem(lane, ROWS) + 1).astype(F32)) & (lane // ROWS == lax.rem(slot, 3)) & (slot < 9)
    pt[...] = jnp.where(hit, 1.0, 0.0).astype(BF16).reshape(512, 128)
    hi, lo = halves(got.reshape(512, 128))
    place = pt[...]

    def placed(x):
        return lax.dot_general(place, x, (((0,), (0,)), ((), ())), preferred_element_type=F32)

    force = placed(hi) + placed(lo)
    fext[:, pl.ds(8, ROWS), :] = force[:ENT].reshape(3, ROWS, 128)
    send(fext.at[:, pl.ds(ROWS, 8), :], fext.at[:, pl.ds(0, 8), :], 9, nxt_id)
    send(fext.at[:, pl.ds(8, 8), :], fext.at[:, pl.ds(ROWS + 8, 8), :], 10, prv_id)

    taken(gin1.at[pl.ds(0, 7)], rsem.at[6])
    total = gin1[0]
    for g in range(1, 8):
        total = total + gin1[g]
    gsum1[...] = total
    gin2[chip] = total
    reduce_far(gsum1, gin2, 7)

    for i in (2, 3):
        taken(dbuf.at[:, pl.ds(0, 8), :], rsem.at[i])
    for i in (4, 5):
        taken(sbuf.at[pl.ds(0, 8), :], rsem.at[i])
    for i in (9, 10):
        taken(fext.at[:, pl.ds(0, 8), :], rsem.at[i])

    long = ROWS + 16
    at_row = iota((3, long, 128), 1) + me * ROWS - 8
    inside = (at_row >= 0) & (at_row < ND * ROWS)
    inverse = jnp.where(inside, 1.0 / (4.0 + sbuf[...])[None], 0.0)
    loads = jnp.where(inside, fext[...], 0.0)
    solved = jnp.where(inside, dbuf[...], 0.0)
    start = solved[:, 8 : 8 + ROWS]
    q = iota((3, long, 128), 2)
    for _ in range(SWEEPS):
        zero = jnp.zeros((3, 1, 128), F32)
        up = jnp.concatenate([zero, solved[:, : long - 1]], axis=1)
        down = jnp.concatenate([solved[:, 1:], zero], axis=1)
        left = jnp.where(q == 0, 0.0, pltpu.roll(solved, 1, 2))
        right = jnp.where(q == 127, 0.0, pltpu.roll(solved, 127, 2))
        solved = (loads + ((up + down) + (left + right))) * inverse
    solved = solved[:, 8 : 8 + ROWS]
    residual = (solved - start).reshape(ENT, 128)
    solved = solved.reshape(ENT, 128)

    resid[...] = residual

    def project(t, accs):
        accs = list(accs)
        for u in range(48):
            i = t * 48 + u
            accs[u % 4] = accs[u % 4] + history(i) * resid[pl.ds(i, 1), :]
        return tuple(accs)

    accs = lax.fori_loop(0, 2, project, (jnp.zeros((HIST, 128), F32),) * 4)
    proj = (accs[0] + accs[1]) + (accs[2] + accs[3])
    square = jnp.sum((residual * residual).reshape(ENT // 8, 8, 128), axis=0)
    sums = jnp.concatenate([proj, square, jnp.zeros((128 - HIST - 8, 128), F32)], axis=0)
    hi = sums.astype(BF16)
    rest = sums - hi.astype(F32)
    mid, low = halves(rest)
    one8 = jnp.ones((16, 128), BF16)
    line = (dot_t(one8, hi) + dot_t(one8, mid) + dot_t(one8, low))[:1]
    psend[...] = line
    pin[me] = line

    def tell(d, carry):
        other = lax.rem(me + d, ND)
        send(psend, pin.at[me], 11, (other // NS, lax.rem(other, NS)))
        return carry

    lax.fori_loop(1, ND, tell, 0)

    taken(gin2.at[pl.ds(0, 15)], rsem.at[7])
    total = gin2[0]
    for g in range(1, 16):
        total = total + gin2[g]
    half = jnp.concatenate([total[:, :HIST], total[:, HIST:]], axis=0)
    work = jnp.concatenate([half + half.T, jnp.where(eye, 1.0, 0.0)], axis=1)
    sub64 = iota((HIST, 128), 0)

    def eliminate(work, first, last):
        for k in range(first, last):
            pivot = work[k : k + 1, :] * (1.0 / work[k : k + 1, k : k + 1])
            work = jnp.where(sub64 == k, pivot, work - work[:, k : k + 1] * pivot)
        return work
    work = eliminate(work, 0, HIST)
    l_w.wait()

    taken(pin.at[pl.ds(0, ND - 1)], rsem.at[11])
    total = jnp.sum(pin[...], axis=0)
    weights = -jnp.sum(work[:, HIST:] * total[0:1, :HIST], axis=1, keepdims=True)
    cbuf[...] = jnp.broadcast_to(weights, (HIST, 128))
    lane1 = iota((1, 128), 1)
    squares = jnp.sum(jnp.where((lane1 >= HIST) & (lane1 < HIST + 8), total, 0.0), axis=1, keepdims=True)
    norm[...] = jnp.sqrt(squares)

    def update(t, acc):
        for u in range(8):
            j = t * 8 + u
            acc = acc + cbuf[pl.ds(j, 1), :] * wv[pl.ds(pl.multiple_of(j * ENT, 8), ENT), :]
        return acc

    moved = solved + lax.fori_loop(0, HIST // 8, update, jnp.zeros((ENT, 128), F32))
    nd[...] = moved

    shell = jnp.concatenate([moved, jnp.zeros((128 - ENT, 128), F32)], axis=0).astype(BF16)
    rep[...] = dot(pt[...], shell).astype(BF16).reshape(NF, SLOTS, 128)
    exchange(rep, back, 12)
    taken(back, rsem.at[12])
    local[...] = dot(oht[...], back[...].reshape(512, 128)).astype(BF16)

    for i, ref in (
        (0, fbuf.at[:, pl.ds(0, EDGE), :]), (1, fbuf.at[:, pl.ds(0, EDGE), :]),
        (2, dbuf.at[:, pl.ds(0, 8), :]), (3, dbuf.at[:, pl.ds(0, 8), :]),
        (4, sbuf.at[pl.ds(0, 8), :]), (5, sbuf.at[pl.ds(0, 8), :]),
        (6, gin1.at[pl.ds(0, 7)]), (7, gin2.at[pl.ds(0, 15)]),
        (8, arrived.at[pl.ds(0, NF - 1)]),
        (9, fext.at[:, pl.ds(0, 8), :]), (10, fext.at[:, pl.ds(0, 8), :]),
        (11, pin.at[pl.ds(0, ND - 1)]),
        (12, back.at[pl.ds(0, NF - 1)]),
    ):
        taken(ref, ssem.at[i])


def finish(nf, nd, local, norm, rbv, nf_out, nd_out, wn_out, norm_out, wn, sems):
    copies = [pltpu.make_async_copy(nf.at[k], nf_out.at[k], sems.at[k]) for k in range(3)]
    copies.append(pltpu.make_async_copy(nd, nd_out, sems.at[3]))
    copies.append(pltpu.make_async_copy(norm, norm_out, sems.at[4]))
    for copy in copies:
        copy.start()
    for i in range(4):
        for u in range(16):
            b = i * 16 + u
            wn[:, b * BLK : (b + 1) * BLK] = dot_t(local[b * 8 : b * 8 + 8, :], rbv[b])[:3]
        points = pl.ds(i * 16 * BLK, 16 * BLK)
        copies.append(pltpu.make_async_copy(wn.at[:, points], wn_out.at[:, points], sems.at[5 + i]))
        copies[-1].start()
    for copy in copies:
        copy.wait()


def per_device(flow, wm, aop, wc, ws, rbf, owner, row, disp, stiff, vh, wh):
    any_ = pl.BlockSpec(memory_space=pl.ANY)
    vmem = pl.BlockSpec(memory_space=pltpu.VMEM)
    out = pl.pallas_call(
        kernel,
        name="coupling",
        out_shape=(
            pltpu.VMEM((3, POINTS, 128), BF16),
            pltpu.VMEM((ENT, 128), F32),
            pltpu.VMEM((BLOCKS * 8, 128), BF16),
            pltpu.VMEM((1, 1), F32),
            pltpu.VMEM((BLOCKS, BLK, 128), BF16),
        ),
        in_specs=[pl.BlockSpec(memory_space=pltpu.HBM)] * 12,
        out_specs=(vmem,) * 5,
        scratch_shapes=[
            pltpu.VMEM((3, POINTS + 2 * EDGE, 128), BF16),
            pltpu.VMEM((3, POINTS), F32),
            pltpu.VMEM((128, 128), BF16),
            pltpu.VMEM((1, 128), F32),
            pltpu.VMEM((1, 128), BF16),
            pltpu.VMEM((1, BLOCKS), jnp.int32),
            pltpu.VMEM((1, BLOCKS), jnp.int32),
            pltpu.VMEM((3, ROWS + 16, 128), F32),
            pltpu.VMEM((ROWS + 16, 128), F32),
            pltpu.VMEM((HIST * ENT, 128), F32),
            pltpu.VMEM((HIST * ENT, 128), F32),
            pltpu.VMEM((BLOCKS * 8, 128), F32),
            pltpu.VMEM((512, 512), BF16),
            pltpu.VMEM((512, 512), BF16),
            pltpu.VMEM((BLOCKS, 128), F32),
            pltpu.VMEM((32, 128), F32),
            pltpu.VMEM((8, 32, 128), F32),
            pltpu.VMEM((32, 128), F32),
            pltpu.VMEM((16, 32, 128), F32),
            pltpu.VMEM((NF, SLOTS, 128), F32),
            pltpu.VMEM((NF, SLOTS, 128), F32),
            pltpu.VMEM((512, 128), BF16),
            pltpu.VMEM((3, ROWS + 16, 128), F32),
            pltpu.VMEM((1, 128), F32),
            pltpu.VMEM((ND, 1, 128), F32),
            pltpu.VMEM((HIST, 128), F32),
            pltpu.VMEM((NF, SLOTS, 128), BF16),
            pltpu.VMEM((NF, SLOTS, 128), BF16),
            pltpu.VMEM((ENT, 128), F32),
            pltpu.VMEM((24, BLK + 2 * EDGE, 128), F32),
            pltpu.VMEM((BLOCKS, 16, 128), BF16),
            pltpu.SemaphoreType.DMA((11 + CHUNKS,)),
            pltpu.SemaphoreType.DMA((13,)),
            pltpu.SemaphoreType.DMA((13,)),
        ],
        compiler_params=pltpu.CompilerParams(
            collective_id=0, has_side_effects=True, vmem_limit_bytes=55 << 20
        ),
    )(
        flow, wm, aop, wc.reshape(1, 128), ws.reshape(1, 128), rbf,
        owner.reshape(1, BLOCKS), row.reshape(1, BLOCKS),
        jnp.transpose(disp, (1, 0, 2)), stiff,
        jnp.transpose(vh, (0, 2, 1, 3)).reshape(HIST * ENT, 128),
        jnp.transpose(wh, (0, 2, 1, 3)).reshape(HIST * ENT, 128),
    )
    new_flow, moved, wall_next, norm = pl.pallas_call(
        finish,
        name="wall",
        out_shape=(
            jax.ShapeDtypeStruct((3, POINTS, 128), BF16),
            jax.ShapeDtypeStruct((ENT, 128), F32),
            jax.ShapeDtypeStruct((3, POINTS), F32),
            jax.ShapeDtypeStruct((1, 1), F32),
        ),
        in_specs=[vmem, vmem, vmem, any_, vmem],
        out_specs=(any_,) * 4,
        scratch_shapes=[pltpu.VMEM((3, POINTS), F32), pltpu.SemaphoreType.DMA((9,))],
        compiler_params=pltpu.CompilerParams(vmem_limit_bytes=8 << 20),
    )(*out)
    moved = jnp.transpose(moved.reshape(3, ROWS, 128), (1, 0, 2))
    return new_flow, moved, wall_next, norm.reshape(())


def solution(mesh):
    both = ("fluid", "solid")
    return jax.shard_map(
        per_device,
        mesh=mesh,
        in_specs=(
            P(None, both, None), P(None, both), P(), P(), P(), P(both, None, None), P(both, None), P(both, None),
            P(both, None, None), P(both, None), P(None, both, None, None), P(None, both, None, None),
        ),
        out_specs=(P(None, both, None), P(both, None, None), P(None, both), P()),
        check_vma=False,
    )
```

```python
import jax
import jax.numpy as jnp
from jax import lax
from jax.experimental import pallas as pl
from jax.experimental.pallas import tpu as pltpu
from jax.sharding import PartitionSpec as P

MESH = pl.DeviceIdType.MESH
F32 = jnp.float32
BF16 = jnp.bfloat16
SWEEPS = 4
NF = 32
NS = 4
ND = NF * NS
BLOCKS = 64
BLK = 128
POINTS = BLOCKS * BLK
EDGE = 16
CHUNKS = 8
ROWS = 32
HIST = 64
ENT = 96
SLOTS = 16


def iota(shape, dim):
    return lax.broadcasted_iota(jnp.int32, shape, dim)


def dot(a, b):
    return jnp.dot(a, b, preferred_element_type=F32)


def dot_t(a, b):
    return lax.dot_general(a, b, (((1,), (1,)), ((), ())), preferred_element_type=F32)


def halves(x):
    hi = x.astype(BF16)
    return hi, (x - hi.astype(F32)).astype(BF16)


def kernel(
    flow, wm, aop, wc, ws, rbf, owner, row, disp, stiff, vh, wh,
    nf, nd, local, norm, rbv,
    fbuf, wmv, av, wcv, wsv, ownv, rowv, dbuf, sbuf, vv, wv,
    mapped, oh, oht, lab, gsend, gin1, gsum1, gin2, out, arrived, pt, fext,
    psend, pin, cbuf, rep, back, resid, late, wide32, tract,
    lsem, ssem, rsem,
):
    f, s = lax.axis_index("fluid"), lax.axis_index("solid")
    me = f * NS + s
    nxt, prv = lax.rem(me + 1, ND), lax.rem(me + ND - 1, ND)
    nxt_id, prv_id = (nxt // NS, lax.rem(nxt, NS)), (prv // NS, lax.rem(prv, NS))
    core, chip = lax.rem(f, 2), f // 2
    near = core * NS + s

    def near_id(d):
        other = lax.rem(near + d, 8)
        return other, (chip * 2 + other // NS, lax.rem(other, NS))

    def far_id(d):
        other = lax.rem(chip + d, 16)
        return other, (other * 2 + core, s)

    barrier = pltpu.get_barrier_semaphore()

    def signal(device):
        pl.semaphore_signal(barrier, inc=1, device_id=device, device_id_type=MESH)

    def greet_fluid(d, carry):
        signal((lax.rem(f + d, NF), s))
        return carry

    lax.fori_loop(1, NF, greet_fluid, 0)

    def greet_near(d, carry):
        signal(near_id(d)[1])
        return carry

    lax.fori_loop(1, 8, greet_near, 0)
    signal(nxt_id)
    signal(prv_id)

    def load(src, dst, i):
        copy = pltpu.make_async_copy(src, dst, lsem.at[i])
        copy.start()
        return copy

    part = POINTS // CHUNKS
    l_a = load(aop, av, 3)
    l_wc = load(wc, wcv, 4)
    l_ws = load(ws, wsv, 5)
    l_wm = load(wm, wmv, 6)
    l_flow = [
        load(flow.at[:, pl.ds(i * part, part), :], fbuf.at[:, pl.ds(EDGE + i * part, part), :], 9 + i)
        for i in range(CHUNKS)
    ]
    l_own = load(owner, ownv, 0)
    l_row = load(row, rowv, 1)
    l_disp = load(disp, dbuf.at[:, pl.ds(8, ROWS), :], 7)
    l_stiff = load(stiff, sbuf.at[pl.ds(8, ROWS), :], 8)
    l_rbf = load(rbf, rbv, 9 + CHUNKS)
    l_v = load(vh, vv, 2)
    l_w = load(wh, wv, 10 + CHUNKS)

    def send(src, dst, i, device):
        pltpu.make_async_remote_copy(
            src_ref=src, dst_ref=dst, send_sem=ssem.at[i], recv_sem=rsem.at[i],
            device_id=device, device_id_type=MESH,
        ).start()

    def taken(ref, sem):
        pltpu.make_async_copy(ref, ref, sem).wait()

    def reduce_near(src, dst, i):
        def step(d, carry):
            send(src, dst.at[near], i, near_id(d)[1])
            return carry

        lax.fori_loop(1, 8, step, 0)

    def reduce_far(src, dst, i):
        def step(d, carry):
            send(src, dst.at[chip], i, far_id(d)[1])
            return carry

        lax.fori_loop(1, 16, step, 0)

    l_a.wait()
    l_wc.wait()
    l_ws.wait()
    l_wm.wait()
    a = av[...]
    coupling = wcv[...]

    stencil = jnp.concatenate([jnp.broadcast_to(wsv[...].astype(F32), (16, 128))] * 3, axis=1)
    stencil = jnp.where(iota((16, 384), 1) // 128 == iota((16, 384), 0), stencil, 0.0).astype(BF16)
    sub = iota((8, 128), 0)

    def slab(b, u):
        base = pl.multiple_of(b * BLK, BLK)
        for c in range(3):
            ext = fbuf[c, pl.ds(base, BLK + 2 * EDGE), :]
            e = wide32.at[u * 3 + c]
            e[...] = ext.astype(F32)
            near_by = e[pl.ds(EDGE - 1, BLK), :] + e[pl.ds(EDGE + 1, BLK), :]
            drift = dot(ext[EDGE : EDGE + BLK], a)
            motion = jnp.broadcast_to(wmv[c : c + 1, pl.ds(base, BLK)], (BLK, 128)).T
            new = 0.5 * e[pl.ds(EDGE, BLK), :] + 0.25 * near_by + drift + motion * coupling
            nf[c, pl.ds(base, BLK), :] = new.astype(BF16)

    def slab_step(i, carry):
        for u in range(8):
            slab(i * 8 + u, u)
        return carry

    def pull(points):
        x = jnp.concatenate([nf[c, points, :] for c in range(3)], axis=1)
        return dot_t(stencil, x).astype(BF16)

    def spread_out(b, tractions):
        m = dot(tractions, rbv[b])[:8]
        m = jnp.where(sub < 3, m, jnp.where(sub == 3, lab[pl.ds(b, 1), :], 0.0))
        mapped[pl.ds(pl.multiple_of(b * 8, 8), 8), :] = m

    def pull_step(i, carry):
        t = pull(pl.ds(pl.multiple_of(i * 16 * BLK, BLK), 16 * BLK))
        for u in range(16):
            tract[i * 16 + u] = t[:, u * 128 : (u + 1) * 128]
        return carry

    def map_step(i, carry):
        for u in range(16):
            spread_out(i * 16 + u, tract[i * 16 + u])
        return carry

    ends = (0, BLOCKS - 1)
    for b in ends:
        nf[:, b * BLK : (b + 1) * BLK, :] = jnp.zeros((3, BLK, 128), BF16)
    l_flow[0].wait()
    l_flow[1].wait()
    for u in range(1, 8):
        slab(u, u)
    for i in range(1, CHUNKS - 1):
        l_flow[i + 1].wait()
        lax.fori_loop(i, i + 1, slab_step, 0)
    for u in range(7):
        slab(BLOCKS - 8 + u, u)

    pl.semaphore_wait(barrier, NF - 1 + 7 + 2)

    l_disp.wait()
    l_stiff.wait()
    send(flow.at[:, pl.ds(POINTS - EDGE, EDGE), :], fbuf.at[:, pl.ds(0, EDGE), :], 0, nxt_id)
    send(flow.at[:, pl.ds(0, EDGE), :], fbuf.at[:, pl.ds(EDGE + POINTS, EDGE), :], 1, prv_id)
    send(dbuf.at[:, pl.ds(ROWS, 8), :], dbuf.at[:, pl.ds(0, 8), :], 2, nxt_id)
    send(dbuf.at[:, pl.ds(8, 8), :], dbuf.at[:, pl.ds(ROWS + 8, 8), :], 3, prv_id)
    send(sbuf.at[pl.ds(ROWS, 8), :], sbuf.at[pl.ds(0, 8), :], 4, nxt_id)
    send(sbuf.at[pl.ds(8, 8), :], sbuf.at[pl.ds(ROWS + 8, 8), :], 5, prv_id)

    lax.fori_loop(0, BLOCKS // 16, pull_step, 0)

    l_own.wait()
    l_row.wait()
    own_row = ownv[...].astype(F32)
    lab_row = rowv[...].astype(F32)
    eye = iota((HIST, HIST), 0) == iota((HIST, HIST), 1)
    ones = jnp.ones((BLOCKS, 128), BF16)
    own_col = dot(jnp.where(eye, own_row, 0.0).astype(BF16), ones)
    lab[...] = dot(jnp.where(eye, lab_row, 0.0).astype(BF16), ones) + 1.0
    same = own_col[:, :BLOCKS] == own_row
    above = iota((BLOCKS, BLOCKS), 0) < iota((BLOCKS, BLOCKS), 1)
    before_row = jnp.sum(jnp.where(same & above, 1.0, 0.0), axis=0, keepdims=True)
    below = iota((BLOCKS, BLOCKS), 1) < iota((BLOCKS, BLOCKS), 0)
    before_col = dot(jnp.where(same & below, 1.0, 0.0).astype(BF16), ones)
    both = jnp.where(iota((16, BLOCKS), 0) == 0, own_row, before_row).astype(BF16)
    wide = dot(both, jnp.where(iota((BLOCKS, 512), 1) // 8 == iota((BLOCKS, 512), 0), 1.0, 0.0).astype(BF16))

    def target(own, before, comp):
        return own * SLOTS + jnp.where(comp < 3.0, before * 3.0 + comp, jnp.where(comp == 3.0, 9.0 + before, -1e6))

    tgt_row = target(wide[0:1], wide[1:2], lax.rem(iota((1, 512), 1), 8).astype(F32))
    oh[...] = jnp.where(iota((512, 512), 0).astype(F32) == tgt_row, 1.0, 0.0).astype(BF16)
    tall = jnp.where(iota((512, BLOCKS), 0) // 8 == iota((512, BLOCKS), 1), 1.0, 0.0).astype(BF16)
    tgt_col = target(
        dot(tall, own_col.astype(BF16)),
        dot(tall, before_col.astype(BF16)),
        lax.rem(iota((512, 128), 0), 8).astype(F32),
    )
    for t in range(4):
        oht[:, t * 128 : (t + 1) * 128] = jnp.where(
            (iota((512, 128), 1) + t * 128).astype(F32) == tgt_col, 1.0, 0.0
        ).astype(BF16)

    l_rbf.wait()
    lax.fori_loop(0, BLOCKS // 16, map_step, 0)

    taken(fbuf.at[:, pl.ds(0, EDGE), :], rsem.at[0])
    taken(fbuf.at[:, pl.ds(0, EDGE), :], rsem.at[1])

    @pl.when(me == 0)
    def _():
        fbuf[:, 0:EDGE, :] = jnp.zeros((3, EDGE, 128), BF16)

    @pl.when(me == ND - 1)
    def _():
        fbuf[:, EDGE + POINTS :, :] = jnp.zeros((3, EDGE, 128), BF16)

    for u, b in enumerate(ends):
        slab(b, u)
    for b in ends:
        spread_out(b, pull(pl.ds(b * BLK, BLK)))

    hi, lo = halves(mapped[...])
    out[...] = (dot(oh[...], hi) + dot(oh[...], lo)).reshape(NF, SLOTS, 128)

    def exchange(src, dst, i):
        def step(d, carry):
            other = lax.rem(f + d, NF)
            send(src.at[other], dst.at[f], i, (other, s))
            return carry

        lax.fori_loop(1, NF, step, 0)
        pltpu.make_async_copy(src.at[f], dst.at[f], rsem.at[i]).start()

    exchange(out, arrived, 8)

    l_v.wait()

    def history(i):
        return vv[pl.ds(i, HIST, stride=ENT), :]

    def gram_step(t, acc):
        for u in range(4):
            i = t * 8 + u * 2
            x = jnp.concatenate([history(i), history(i + 1)], axis=1)
            hi, lo = halves(x)
            acc = acc + dot_t(hi, jnp.concatenate([hi, lo], axis=0))
        return acc

    gram = lax.fori_loop(0, ENT // 8, gram_step, jnp.zeros((HIST, 128), F32))
    half = 0.5 * gram[:, :HIST] + gram[:, HIST:]
    packed = jnp.concatenate([half[:32], half[32:]], axis=1)
    gsend[...] = packed
    gin1[near] = packed
    reduce_near(gsend, gin1, 6)

    taken(arrived, rsem.at[8])
    got = arrived[...]
    slot = iota((NF, SLOTS, 128), 1)
    label = jnp.where(slot < 3, got[:, 9:10], jnp.where(slot < 6, got[:, 10:11], got[:, 11:12]))
    lane = iota((NF, SLOTS, 128), 2)
    hit = (label == (lax.rem(lane, ROWS) + 1).astype(F32)) & (lane // ROWS == lax.rem(slot, 3)) & (slot < 9)
    pt[...] = jnp.where(hit, 1.0, 0.0).astype(BF16).reshape(512, 128)
    hi, lo = halves(got.reshape(512, 128))
    place = pt[...]

    def placed(x):
        return lax.dot_general(place, x, (((0,), (0,)), ((), ())), preferred_element_type=F32)

    force = placed(hi) + placed(lo)
    fext[:, pl.ds(8, ROWS), :] = force[:ENT].reshape(3, ROWS, 128)
    send(fext.at[:, pl.ds(ROWS, 8), :], fext.at[:, pl.ds(0, 8), :], 9, nxt_id)
    send(fext.at[:, pl.ds(8, 8), :], fext.at[:, pl.ds(ROWS + 8, 8), :], 10, prv_id)

    taken(gin1.at[pl.ds(0, 7)], rsem.at[6])
    total = gin1[0]
    for g in range(1, 8):
        total = total + gin1[g]
    gsum1[...] = total
    gin2[chip] = total
    reduce_far(gsum1, gin2, 7)

    for i in (2, 3):
        taken(dbuf.at[:, pl.ds(0, 8), :], rsem.at[i])
    for i in (4, 5):
        taken(sbuf.at[pl.ds(0, 8), :], rsem.at[i])

    long = ROWS + 16
    at_row = iota((3, long, 128), 1) + me * ROWS - 8
    inside = (at_row >= 0) & (at_row < ND * ROWS)
    inverse = jnp.where(inside, 1.0 / (4.0 + sbuf[...])[None], 0.0)
    begin = jnp.where(inside, dbuf[...], 0.0)
    q = iota((3, long, 128), 2)

    def sweep(loads):
        solved = begin
        for _ in range(SWEEPS):
            zero = jnp.zeros((3, 1, 128), F32)
            up = jnp.concatenate([zero, solved[:, : long - 1]], axis=1)
            down = jnp.concatenate([solved[:, 1:], zero], axis=1)
            left = jnp.where(q == 0, 0.0, pltpu.roll(solved, 1, 2))
            right = jnp.where(q == 127, 0.0, pltpu.roll(solved, 127, 2))
            solved = (loads + ((up + down) + (left + right))) * inverse
        solved = solved[:, 8 : 8 + ROWS]
        return solved.reshape(ENT, 128), (solved - begin[:, 8 : 8 + ROWS]).reshape(ENT, 128)

    def project(rows, ref, accs):
        accs = list(accs)
        for n, r in enumerate(rows):
            for c in range(3):
                i = c * ROWS + r
                u = (n * 3 + c) % 4
                accs[u] = accs[u] + history(i) * ref[i : i + 1, :]
        return accs

    none = jnp.zeros((3, 8, 128), F32)
    resid[...] = sweep(jnp.concatenate([none, force[:ENT].reshape(3, ROWS, 128), none], axis=1))[1]
    accs = project(range(3, ROWS - 3), resid, [jnp.zeros((HIST, 128), F32)] * 4)


    for i in (9, 10):
        taken(fext.at[:, pl.ds(0, 8), :], rsem.at[i])

    solved, residual = sweep(jnp.where(inside, fext[...], 0.0))
    late[...] = residual
    accs = project(range(3), late, accs)
    accs = project(range(ROWS - 3, ROWS), late, accs)
    proj = (accs[0] + accs[1]) + (accs[2] + accs[3])
    square = jnp.sum((residual * residual).reshape(ENT // 8, 8, 128), axis=0)
    sums = jnp.concatenate([proj, square, jnp.zeros((128 - HIST - 8, 128), F32)], axis=0)
    hi = sums.astype(BF16)
    rest = sums - hi.astype(F32)
    mid, low = halves(rest)
    one8 = jnp.ones((16, 128), BF16)
    line = (dot_t(one8, hi) + dot_t(one8, mid) + dot_t(one8, low))[:1]
    psend[...] = line
    pin[me] = line

    def tell(d, carry):
        other = lax.rem(me + d, ND)
        send(psend, pin.at[me], 11, (other // NS, lax.rem(other, NS)))
        return carry

    lax.fori_loop(1, ND, tell, 0)

    taken(gin2.at[pl.ds(0, 15)], rsem.at[7])
    total = gin2[0]
    for g in range(1, 16):
        total = total + gin2[g]
    half = jnp.concatenate([total[:, :HIST], total[:, HIST:]], axis=0)
    work = jnp.concatenate([half + half.T, jnp.where(eye, 1.0, 0.0)], axis=1)
    sub64 = iota((HIST, 128), 0)

    def eliminate(work, first, last):
        for k in range(first, last):
            pivot = work[k : k + 1, :] * (1.0 / work[k : k + 1, k : k + 1])
            work = jnp.where(sub64 == k, pivot, work - work[:, k : k + 1] * pivot)
        return work
    work = eliminate(work, 0, HIST)
    l_w.wait()

    taken(pin.at[pl.ds(0, ND - 1)], rsem.at[11])
    total = jnp.sum(pin[...], axis=0)
    weights = -jnp.sum(work[:, HIST:] * total[0:1, :HIST], axis=1, keepdims=True)
    cbuf[...] = jnp.broadcast_to(weights, (HIST, 128))
    lane1 = iota((1, 128), 1)
    squares = jnp.sum(jnp.where((lane1 >= HIST) & (lane1 < HIST + 8), total, 0.0), axis=1, keepdims=True)
    norm[...] = jnp.sqrt(squares)

    def update(t, acc):
        for u in range(8):
            j = t * 8 + u
            acc = acc + cbuf[pl.ds(j, 1), :] * wv[pl.ds(pl.multiple_of(j * ENT, 8), ENT), :]
        return acc

    moved = solved + lax.fori_loop(0, HIST // 8, update, jnp.zeros((ENT, 128), F32))
    nd[...] = moved

    shell = jnp.concatenate([moved, jnp.zeros((128 - ENT, 128), F32)], axis=0).astype(BF16)
    rep[...] = dot(pt[...], shell).astype(BF16).reshape(NF, SLOTS, 128)
    exchange(rep, back, 12)
    taken(back, rsem.at[12])
    local[...] = dot(oht[...], back[...].reshape(512, 128)).astype(BF16)

    for i, ref in (
        (0, fbuf.at[:, pl.ds(0, EDGE), :]), (1, fbuf.at[:, pl.ds(0, EDGE), :]),
        (2, dbuf.at[:, pl.ds(0, 8), :]), (3, dbuf.at[:, pl.ds(0, 8), :]),
        (4, sbuf.at[pl.ds(0, 8), :]), (5, sbuf.at[pl.ds(0, 8), :]),
        (6, gin1.at[pl.ds(0, 7)]), (7, gin2.at[pl.ds(0, 15)]),
        (8, arrived.at[pl.ds(0, NF - 1)]),
        (9, fext.at[:, pl.ds(0, 8), :]), (10, fext.at[:, pl.ds(0, 8), :]),
        (11, pin.at[pl.ds(0, ND - 1)]),
        (12, back.at[pl.ds(0, NF - 1)]),
    ):
        taken(ref, ssem.at[i])


def finish(nf, nd, local, norm, rbv, nf_out, nd_out, wn_out, norm_out, wn, sems):
    copies = [pltpu.make_async_copy(nf.at[k], nf_out.at[k], sems.at[k]) for k in range(3)]
    copies.append(pltpu.make_async_copy(nd, nd_out, sems.at[3]))
    copies.append(pltpu.make_async_copy(norm, norm_out, sems.at[4]))
    for copy in copies:
        copy.start()
    for i in range(4):
        for u in range(16):
            b = i * 16 + u
            wn[:, b * BLK : (b + 1) * BLK] = dot_t(local[b * 8 : b * 8 + 8, :], rbv[b])[:3]
        points = pl.ds(i * 16 * BLK, 16 * BLK)
        copies.append(pltpu.make_async_copy(wn.at[:, points], wn_out.at[:, points], sems.at[5 + i]))
        copies[-1].start()
    for copy in copies:
        copy.wait()


def per_device(flow, wm, aop, wc, ws, rbf, owner, row, disp, stiff, vh, wh):
    any_ = pl.BlockSpec(memory_space=pl.ANY)
    vmem = pl.BlockSpec(memory_space=pltpu.VMEM)
    out = pl.pallas_call(
        kernel,
        name="coupling",
        out_shape=(
            pltpu.VMEM((3, POINTS, 128), BF16),
            pltpu.VMEM((ENT, 128), F32),
            pltpu.VMEM((BLOCKS * 8, 128), BF16),
            pltpu.VMEM((1, 1), F32),
            pltpu.VMEM((BLOCKS, BLK, 128), BF16),
        ),
        in_specs=[pl.BlockSpec(memory_space=pltpu.HBM)] * 12,
        out_specs=(vmem,) * 5,
        scratch_shapes=[
            pltpu.VMEM((3, POINTS + 2 * EDGE, 128), BF16),
            pltpu.VMEM((3, POINTS), F32),
            pltpu.VMEM((128, 128), BF16),
            pltpu.VMEM((1, 128), F32),
            pltpu.VMEM((1, 128), BF16),
            pltpu.VMEM((1, BLOCKS), jnp.int32),
            pltpu.VMEM((1, BLOCKS), jnp.int32),
            pltpu.VMEM((3, ROWS + 16, 128), F32),
            pltpu.VMEM((ROWS + 16, 128), F32),
            pltpu.VMEM((HIST * ENT, 128), F32),
            pltpu.VMEM((HIST * ENT, 128), F32),
            pltpu.VMEM((BLOCKS * 8, 128), F32),
            pltpu.VMEM((512, 512), BF16),
            pltpu.VMEM((512, 512), BF16),
            pltpu.VMEM((BLOCKS, 128), F32),
            pltpu.VMEM((32, 128), F32),
            pltpu.VMEM((8, 32, 128), F32),
            pltpu.VMEM((32, 128), F32),
            pltpu.VMEM((16, 32, 128), F32),
            pltpu.VMEM((NF, SLOTS, 128), F32),
            pltpu.VMEM((NF, SLOTS, 128), F32),
            pltpu.VMEM((512, 128), BF16),
            pltpu.VMEM((3, ROWS + 16, 128), F32),
            pltpu.VMEM((1, 128), F32),
            pltpu.VMEM((ND, 1, 128), F32),
            pltpu.VMEM((HIST, 128), F32),
            pltpu.VMEM((NF, SLOTS, 128), BF16),
            pltpu.VMEM((NF, SLOTS, 128), BF16),
            pltpu.VMEM((ENT, 128), F32),
            pltpu.VMEM((ENT, 128), F32),
            pltpu.VMEM((24, BLK + 2 * EDGE, 128), F32),
            pltpu.VMEM((BLOCKS, 16, 128), BF16),
            pltpu.SemaphoreType.DMA((11 + CHUNKS,)),
            pltpu.SemaphoreType.DMA((13,)),
            pltpu.SemaphoreType.DMA((13,)),
        ],
        compiler_params=pltpu.CompilerParams(
            collective_id=0, has_side_effects=True, vmem_limit_bytes=55 << 20
        ),
    )(
        flow, wm, aop, wc.reshape(1, 128), ws.reshape(1, 128), rbf,
        owner.reshape(1, BLOCKS), row.reshape(1, BLOCKS),
        jnp.transpose(disp, (1, 0, 2)), stiff,
        jnp.transpose(vh, (0, 2, 1, 3)).reshape(HIST * ENT, 128),
        jnp.transpose(wh, (0, 2, 1, 3)).reshape(HIST * ENT, 128),
    )
    new_flow, moved, wall_next, norm = pl.pallas_call(
        finish,
        name="wall",
        out_shape=(
            jax.ShapeDtypeStruct((3, POINTS, 128), BF16),
            jax.ShapeDtypeStruct((ENT, 128), F32),
            jax.ShapeDtypeStruct((3, POINTS), F32),
            jax.ShapeDtypeStruct((1, 1), F32),
        ),
        in_specs=[vmem, vmem, vmem, any_, vmem],
        out_specs=(any_,) * 4,
        scratch_shapes=[pltpu.VMEM((3, POINTS), F32), pltpu.SemaphoreType.DMA((9,))],
        compiler_params=pltpu.CompilerParams(vmem_limit_bytes=8 << 20),
    )(*out)
    moved = jnp.transpose(moved.reshape(3, ROWS, 128), (1, 0, 2))
    return new_flow, moved, wall_next, norm.reshape(())


def solution(mesh):
    both = ("fluid", "solid")
    return jax.shard_map(
        per_device,
        mesh=mesh,
        in_specs=(
            P(None, both, None), P(None, both), P(), P(), P(), P(both, None, None), P(both, None), P(both, None),
            P(both, None, None), P(both, None), P(None, both, None, None), P(None, both, None, None),
        ),
        out_specs=(P(None, both, None), P(both, None, None), P(None, both), P()),
        check_vma=False,
    )
```

```python
import jax
import jax.numpy as jnp
from jax import lax
from jax.experimental import pallas as pl
from jax.experimental.pallas import tpu as pltpu
from jax.sharding import PartitionSpec as P

MESH = pl.DeviceIdType.MESH
F32 = jnp.float32
BF16 = jnp.bfloat16
SWEEPS = 4
NF = 32
NS = 4
ND = NF * NS
BLOCKS = 64
BLK = 128
POINTS = BLOCKS * BLK
EDGE = 16
CHUNKS = 8
ROWS = 32
HIST = 64
ENT = 96
SLOTS = 16


def iota(shape, dim):
    return lax.broadcasted_iota(jnp.int32, shape, dim)


def dot(a, b):
    return jnp.dot(a, b, preferred_element_type=F32)


def dot_t(a, b):
    return lax.dot_general(a, b, (((1,), (1,)), ((), ())), preferred_element_type=F32)


def halves(x):
    hi = x.astype(BF16)
    return hi, (x - hi.astype(F32)).astype(BF16)


def kernel(
    flow, wm, aop, wc, ws, rbf, owner, row, disp, stiff, vh, wh,
    nf, nd, local, norm, rbv,
    fbuf, wmv, av, wcv, wsv, ownv, rowv, dbuf, sbuf, vv, wv,
    mapped, oh, oht, lab, gsend, gin1, gsum1, gin2, out, arrived, pt, fext,
    psend, pin, cbuf, rep, back, resid, late, wide32, tract,
    lsem, ssem, rsem,
):
    f, s = lax.axis_index("fluid"), lax.axis_index("solid")
    me = f * NS + s
    nxt, prv = lax.rem(me + 1, ND), lax.rem(me + ND - 1, ND)
    nxt_id, prv_id = (nxt // NS, lax.rem(nxt, NS)), (prv // NS, lax.rem(prv, NS))
    core, chip = lax.rem(f, 2), f // 2
    near = core * NS + s

    def near_id(d):
        other = lax.rem(near + d, 8)
        return other, (chip * 2 + other // NS, lax.rem(other, NS))

    def far_id(d):
        other = lax.rem(chip + d, 16)
        return other, (other * 2 + core, s)

    barrier = pltpu.get_barrier_semaphore()

    def signal(device):
        pl.semaphore_signal(barrier, inc=1, device_id=device, device_id_type=MESH)

    def greet_fluid(d, carry):
        signal((lax.rem(f + d, NF), s))
        return carry

    lax.fori_loop(1, NF, greet_fluid, 0)

    def greet_near(d, carry):
        signal(near_id(d)[1])
        return carry

    lax.fori_loop(1, 8, greet_near, 0)
    signal(nxt_id)
    signal(prv_id)

    def load(src, dst, i):
        copy = pltpu.make_async_copy(src, dst, lsem.at[i])
        copy.start()
        return copy

    part = POINTS // CHUNKS
    l_a = load(aop, av, 3)
    l_wc = load(wc, wcv, 4)
    l_ws = load(ws, wsv, 5)
    l_wm = load(wm, wmv, 6)
    l_flow = [
        load(flow.at[:, pl.ds(i * part, part), :], fbuf.at[:, pl.ds(EDGE + i * part, part), :], 9 + i)
        for i in range(CHUNKS)
    ]
    l_own = load(owner, ownv, 0)
    l_row = load(row, rowv, 1)
    l_disp = load(disp, dbuf.at[:, pl.ds(8, ROWS), :], 7)
    l_stiff = load(stiff, sbuf.at[pl.ds(8, ROWS), :], 8)
    l_rbf = load(rbf, rbv, 9 + CHUNKS)
    l_v = load(vh, vv, 2)
    l_w = load(wh, wv, 10 + CHUNKS)

    def send(src, dst, i, device):
        pltpu.make_async_remote_copy(
            src_ref=src, dst_ref=dst, send_sem=ssem.at[i], recv_sem=rsem.at[i],
            device_id=device, device_id_type=MESH,
        ).start()

    def taken(ref, sem):
        pltpu.make_async_copy(ref, ref, sem).wait()

    def reduce_near(src, dst, i):
        def step(d, carry):
            send(src, dst.at[near], i, near_id(d)[1])
            return carry

        lax.fori_loop(1, 8, step, 0)

    def reduce_far(src, dst, i):
        def step(d, carry):
            send(src, dst.at[chip], i, far_id(d)[1])
            return carry

        lax.fori_loop(1, 16, step, 0)

    l_a.wait()
    l_wc.wait()
    l_ws.wait()
    l_wm.wait()
    a = av[...]
    coupling = wcv[...]

    stencil = jnp.concatenate([jnp.broadcast_to(wsv[...].astype(F32), (16, 128))] * 3, axis=1)
    stencil = jnp.where(iota((16, 384), 1) // 128 == iota((16, 384), 0), stencil, 0.0).astype(BF16)
    sub = iota((8, 128), 0)

    def slab(b, u):
        base = pl.multiple_of(b * BLK, BLK)
        for c in range(3):
            ext = fbuf[c, pl.ds(base, BLK + 2 * EDGE), :]
            e = wide32.at[u * 3 + c]
            e[...] = ext.astype(F32)
            near_by = e[pl.ds(EDGE - 1, BLK), :] + e[pl.ds(EDGE + 1, BLK), :]
            drift = dot(ext[EDGE : EDGE + BLK], a)
            motion = jnp.broadcast_to(wmv[c : c + 1, pl.ds(base, BLK)], (BLK, 128)).T
            new = 0.5 * e[pl.ds(EDGE, BLK), :] + 0.25 * near_by + drift + motion * coupling
            nf[c, pl.ds(base, BLK), :] = new.astype(BF16)

    def slab_step(i, carry):
        for u in range(8):
            slab(i * 8 + u, u)
        return carry

    def pull(points):
        x = jnp.concatenate([nf[c, points, :] for c in range(3)], axis=1)
        return dot_t(stencil, x).astype(BF16)

    def spread_out(b, tractions):
        m = dot(tractions, rbv[b])[:8]
        m = jnp.where(sub < 3, m, jnp.where(sub == 3, lab[pl.ds(b, 1), :], 0.0))
        mapped[pl.ds(pl.multiple_of(b * 8, 8), 8), :] = m

    def pull_step(i, carry):
        t = pull(pl.ds(pl.multiple_of(i * 16 * BLK, BLK), 16 * BLK))
        for u in range(16):
            tract[i * 16 + u] = t[:, u * 128 : (u + 1) * 128]
        return carry

    def map_step(i, carry):
        for u in range(16):
            spread_out(i * 16 + u, tract[i * 16 + u])
        return carry

    ends = (0, BLOCKS - 1)
    for b in ends:
        nf[:, b * BLK : (b + 1) * BLK, :] = jnp.zeros((3, BLK, 128), BF16)
    l_flow[0].wait()
    l_flow[1].wait()
    for u in range(1, 8):
        slab(u, u)
    for i in range(1, CHUNKS - 1):
        l_flow[i + 1].wait()
        lax.fori_loop(i, i + 1, slab_step, 0)
    for u in range(7):
        slab(BLOCKS - 8 + u, u)

    pl.semaphore_wait(barrier, NF - 1 + 7 + 2)

    l_disp.wait()
    l_stiff.wait()
    send(flow.at[:, pl.ds(POINTS - EDGE, EDGE), :], fbuf.at[:, pl.ds(0, EDGE), :], 0, nxt_id)
    send(flow.at[:, pl.ds(0, EDGE), :], fbuf.at[:, pl.ds(EDGE + POINTS, EDGE), :], 1, prv_id)
    send(dbuf.at[:, pl.ds(ROWS, 8), :], dbuf.at[:, pl.ds(0, 8), :], 2, nxt_id)
    send(dbuf.at[:, pl.ds(8, 8), :], dbuf.at[:, pl.ds(ROWS + 8, 8), :], 3, prv_id)
    send(sbuf.at[pl.ds(ROWS, 8), :], sbuf.at[pl.ds(0, 8), :], 4, nxt_id)
    send(sbuf.at[pl.ds(8, 8), :], sbuf.at[pl.ds(ROWS + 8, 8), :], 5, prv_id)

    lax.fori_loop(0, BLOCKS // 16, pull_step, 0)

    l_own.wait()
    l_row.wait()
    own_row = ownv[...].astype(F32)
    lab_row = rowv[...].astype(F32)
    eye = iota((HIST, HIST), 0) == iota((HIST, HIST), 1)
    ones = jnp.ones((BLOCKS, 128), BF16)
    own_col = dot(jnp.where(eye, own_row, 0.0).astype(BF16), ones)
    lab[...] = dot(jnp.where(eye, lab_row, 0.0).astype(BF16), ones) + 1.0
    same = own_col[:, :BLOCKS] == own_row
    above = iota((BLOCKS, BLOCKS), 0) < iota((BLOCKS, BLOCKS), 1)
    before_row = jnp.sum(jnp.where(same & above, 1.0, 0.0), axis=0, keepdims=True)
    below = iota((BLOCKS, BLOCKS), 1) < iota((BLOCKS, BLOCKS), 0)
    before_col = dot(jnp.where(same & below, 1.0, 0.0).astype(BF16), ones)
    both = jnp.where(iota((16, BLOCKS), 0) == 0, own_row, before_row).astype(BF16)
    wide = dot(both, jnp.where(iota((BLOCKS, 512), 1) // 8 == iota((BLOCKS, 512), 0), 1.0, 0.0).astype(BF16))

    def target(own, before, comp):
        return own * SLOTS + jnp.where(comp < 3.0, before * 3.0 + comp, jnp.where(comp == 3.0, 9.0 + before, -1e6))

    tgt_row = target(wide[0:1], wide[1:2], lax.rem(iota((1, 512), 1), 8).astype(F32))
    oh[...] = jnp.where(iota((512, 512), 0).astype(F32) == tgt_row, 1.0, 0.0).astype(BF16)
    tall = jnp.where(iota((512, BLOCKS), 0) // 8 == iota((512, BLOCKS), 1), 1.0, 0.0).astype(BF16)
    tgt_col = target(
        dot(tall, own_col.astype(BF16)),
        dot(tall, before_col.astype(BF16)),
        lax.rem(iota((512, 128), 0), 8).astype(F32),
    )
    for t in range(4):
        oht[:, t * 128 : (t + 1) * 128] = jnp.where(
            (iota((512, 128), 1) + t * 128).astype(F32) == tgt_col, 1.0, 0.0
        ).astype(BF16)

    l_rbf.wait()
    lax.fori_loop(0, BLOCKS // 16, map_step, 0)

    taken(fbuf.at[:, pl.ds(0, EDGE), :], rsem.at[0])
    taken(fbuf.at[:, pl.ds(0, EDGE), :], rsem.at[1])

    @pl.when(me == 0)
    def _():
        fbuf[:, 0:EDGE, :] = jnp.zeros((3, EDGE, 128), BF16)

    @pl.when(me == ND - 1)
    def _():
        fbuf[:, EDGE + POINTS :, :] = jnp.zeros((3, EDGE, 128), BF16)

    for u, b in enumerate(ends):
        slab(b, u)
    for b in ends:
        spread_out(b, pull(pl.ds(b * BLK, BLK)))

    hi, lo = halves(mapped[...])
    out[...] = (dot(oh[...], hi) + dot(oh[...], lo)).reshape(NF, SLOTS, 128)

    def exchange(src, dst, i):
        def step(d, carry):
            other = lax.rem(f + d, NF)
            send(src.at[other], dst.at[f], i, (other, s))
            return carry

        lax.fori_loop(1, NF, step, 0)
        pltpu.make_async_copy(src.at[f], dst.at[f], rsem.at[i]).start()

    exchange(out, arrived, 8)

    l_v.wait()

    def history(i):
        return vv[pl.ds(i, HIST, stride=ENT), :]

    def gram_step(t, acc):
        for u in range(4):
            i = t * 8 + u * 2
            x = jnp.concatenate([history(i), history(i + 1)], axis=1)
            hi, lo = halves(x)
            acc = acc + dot_t(hi, jnp.concatenate([hi, lo], axis=0))
        return acc

    gram = lax.fori_loop(0, ENT // 8, gram_step, jnp.zeros((HIST, 128), F32))
    half = 0.5 * gram[:, :HIST] + gram[:, HIST:]
    packed = jnp.concatenate([half[:32], half[32:]], axis=1)
    gsend[...] = packed
    gin1[near] = packed
    reduce_near(gsend, gin1, 6)

    taken(arrived, rsem.at[8])
    got = arrived[...]
    slot = iota((NF, SLOTS, 128), 1)
    label = jnp.where(slot < 3, got[:, 9:10], jnp.where(slot < 6, got[:, 10:11], got[:, 11:12]))
    lane = iota((NF, SLOTS, 128), 2)
    hit = (label == (lax.rem(lane, ROWS) + 1).astype(F32)) & (lane // ROWS == lax.rem(slot, 3)) & (slot < 9)
    pt[...] = jnp.where(hit, 1.0, 0.0).astype(BF16).reshape(512, 128)
    hi, lo = halves(got.reshape(512, 128))
    place = pt[...]

    def placed(x):
        return lax.dot_general(place, x, (((0,), (0,)), ((), ())), preferred_element_type=F32)

    force = placed(hi) + placed(lo)
    fext[:, pl.ds(8, ROWS), :] = force[:ENT].reshape(3, ROWS, 128)
    send(fext.at[:, pl.ds(ROWS, 8), :], fext.at[:, pl.ds(0, 8), :], 9, nxt_id)
    send(fext.at[:, pl.ds(8, 8), :], fext.at[:, pl.ds(ROWS + 8, 8), :], 10, prv_id)

    taken(gin1.at[pl.ds(0, 7)], rsem.at[6])
    total = gin1[0]
    for g in range(1, 8):
        total = total + gin1[g]
    gsum1[...] = total
    gin2[chip] = total
    reduce_far(gsum1, gin2, 7)

    for i in (2, 3):
        taken(dbuf.at[:, pl.ds(0, 8), :], rsem.at[i])
    for i in (4, 5):
        taken(sbuf.at[pl.ds(0, 8), :], rsem.at[i])

    long = ROWS + 16
    at_row = iota((3, long, 128), 1) + me * ROWS - 8
    inside = (at_row >= 0) & (at_row < ND * ROWS)
    inverse = jnp.where(inside, 1.0 / (4.0 + sbuf[...])[None], 0.0)
    begin = jnp.where(inside, dbuf[...], 0.0)
    q = iota((3, long, 128), 2)

    def sweep(loads):
        solved = begin
        for _ in range(SWEEPS):
            zero = jnp.zeros((3, 1, 128), F32)
            up = jnp.concatenate([zero, solved[:, : long - 1]], axis=1)
            down = jnp.concatenate([solved[:, 1:], zero], axis=1)
            left = jnp.where(q == 0, 0.0, pltpu.roll(solved, 1, 2))
            right = jnp.where(q == 127, 0.0, pltpu.roll(solved, 127, 2))
            solved = (loads + ((up + down) + (left + right))) * inverse
        solved = solved[:, 8 : 8 + ROWS]
        return solved.reshape(ENT, 128), (solved - begin[:, 8 : 8 + ROWS]).reshape(ENT, 128)

    def project(rows, ref, accs):
        accs = list(accs)
        for n, r in enumerate(rows):
            for c in range(3):
                i = c * ROWS + r
                u = (n * 3 + c) % 4
                accs[u] = accs[u] + history(i) * ref[i : i + 1, :]
        return accs

    none = jnp.zeros((3, 8, 128), F32)
    resid[...] = sweep(jnp.concatenate([none, force[:ENT].reshape(3, ROWS, 128), none], axis=1))[1]
    accs = project(range(3, ROWS - 3), resid, [jnp.zeros((HIST, 128), F32)] * 4)


    for i in (9, 10):
        taken(fext.at[:, pl.ds(0, 8), :], rsem.at[i])

    solved, residual = sweep(jnp.where(inside, fext[...], 0.0))
    late[...] = residual
    accs = project(range(3), late, accs)
    accs = project(range(ROWS - 3, ROWS), late, accs)
    proj = (accs[0] + accs[1]) + (accs[2] + accs[3])
    square = jnp.sum((residual * residual).reshape(ENT // 8, 8, 128), axis=0)
    sums = jnp.concatenate([proj, square, jnp.zeros((128 - HIST - 8, 128), F32)], axis=0)
    hi = sums.astype(BF16)
    rest = sums - hi.astype(F32)
    mid, low = halves(rest)
    one8 = jnp.ones((16, 128), BF16)
    line = (dot_t(one8, hi) + dot_t(one8, mid) + dot_t(one8, low))[:1]
    psend[...] = line
    pin[me] = line

    def tell(k, carry):
        other = lax.rem(me + ND + (1 - 2 * lax.rem(k, 2)) * (k // 2 + 1), ND)
        send(psend, pin.at[me], 11, (other // NS, lax.rem(other, NS)))
        return carry

    lax.fori_loop(0, ND - 1, tell, 0)

    taken(gin2.at[pl.ds(0, 15)], rsem.at[7])
    total = gin2[0]
    for g in range(1, 16):
        total = total + gin2[g]
    half = jnp.concatenate([total[:, :HIST], total[:, HIST:]], axis=0)
    work = jnp.concatenate([half + half.T, jnp.where(eye, 1.0, 0.0)], axis=1)
    sub64 = iota((HIST, 128), 0)

    def eliminate(work, first, last):
        for k in range(first, last):
            pivot = work[k : k + 1, :] * (1.0 / work[k : k + 1, k : k + 1])
            work = jnp.where(sub64 == k, pivot, work - work[:, k : k + 1] * pivot)
        return work
    work = eliminate(work, 0, HIST)
    l_w.wait()

    taken(pin.at[pl.ds(0, ND - 1)], rsem.at[11])
    total = jnp.sum(pin[...], axis=0)
    weights = -jnp.sum(work[:, HIST:] * total[0:1, :HIST], axis=1, keepdims=True)
    cbuf[...] = jnp.broadcast_to(weights, (HIST, 128))
    lane1 = iota((1, 128), 1)
    squares = jnp.sum(jnp.where((lane1 >= HIST) & (lane1 < HIST + 8), total, 0.0), axis=1, keepdims=True)
    norm[...] = jnp.sqrt(squares)

    def update(t, acc):
        for u in range(8):
            j = t * 8 + u
            acc = acc + cbuf[pl.ds(j, 1), :] * wv[pl.ds(pl.multiple_of(j * ENT, 8), ENT), :]
        return acc

    moved = solved + lax.fori_loop(0, HIST // 8, update, jnp.zeros((ENT, 128), F32))
    nd[...] = moved

    shell = jnp.concatenate([moved, jnp.zeros((128 - ENT, 128), F32)], axis=0).astype(BF16)
    rep[...] = dot(pt[...], shell).astype(BF16).reshape(NF, SLOTS, 128)
    exchange(rep, back, 12)
    taken(back, rsem.at[12])
    local[...] = dot(oht[...], back[...].reshape(512, 128)).astype(BF16)

    for i, ref in (
        (0, fbuf.at[:, pl.ds(0, EDGE), :]), (1, fbuf.at[:, pl.ds(0, EDGE), :]),
        (2, dbuf.at[:, pl.ds(0, 8), :]), (3, dbuf.at[:, pl.ds(0, 8), :]),
        (4, sbuf.at[pl.ds(0, 8), :]), (5, sbuf.at[pl.ds(0, 8), :]),
        (6, gin1.at[pl.ds(0, 7)]), (7, gin2.at[pl.ds(0, 15)]),
        (8, arrived.at[pl.ds(0, NF - 1)]),
        (9, fext.at[:, pl.ds(0, 8), :]), (10, fext.at[:, pl.ds(0, 8), :]),
        (11, pin.at[pl.ds(0, ND - 1)]),
        (12, back.at[pl.ds(0, NF - 1)]),
    ):
        taken(ref, ssem.at[i])


def finish(nf, nd, local, norm, rbv, nf_out, nd_out, wn_out, norm_out, wn, sems):
    copies = [pltpu.make_async_copy(nf.at[k], nf_out.at[k], sems.at[k]) for k in range(3)]
    copies.append(pltpu.make_async_copy(nd, nd_out, sems.at[3]))
    copies.append(pltpu.make_async_copy(norm, norm_out, sems.at[4]))
    for copy in copies:
        copy.start()
    for i in range(4):
        for u in range(16):
            b = i * 16 + u
            wn[:, b * BLK : (b + 1) * BLK] = dot_t(local[b * 8 : b * 8 + 8, :], rbv[b])[:3]
        points = pl.ds(i * 16 * BLK, 16 * BLK)
        copies.append(pltpu.make_async_copy(wn.at[:, points], wn_out.at[:, points], sems.at[5 + i]))
        copies[-1].start()
    for copy in copies:
        copy.wait()


def per_device(flow, wm, aop, wc, ws, rbf, owner, row, disp, stiff, vh, wh):
    any_ = pl.BlockSpec(memory_space=pl.ANY)
    vmem = pl.BlockSpec(memory_space=pltpu.VMEM)
    out = pl.pallas_call(
        kernel,
        name="coupling",
        out_shape=(
            pltpu.VMEM((3, POINTS, 128), BF16),
            pltpu.VMEM((ENT, 128), F32),
            pltpu.VMEM((BLOCKS * 8, 128), BF16),
            pltpu.VMEM((1, 1), F32),
            pltpu.VMEM((BLOCKS, BLK, 128), BF16),
        ),
        in_specs=[pl.BlockSpec(memory_space=pltpu.HBM)] * 12,
        out_specs=(vmem,) * 5,
        scratch_shapes=[
            pltpu.VMEM((3, POINTS + 2 * EDGE, 128), BF16),
            pltpu.VMEM((3, POINTS), F32),
            pltpu.VMEM((128, 128), BF16),
            pltpu.VMEM((1, 128), F32),
            pltpu.VMEM((1, 128), BF16),
            pltpu.VMEM((1, BLOCKS), jnp.int32),
            pltpu.VMEM((1, BLOCKS), jnp.int32),
            pltpu.VMEM((3, ROWS + 16, 128), F32),
            pltpu.VMEM((ROWS + 16, 128), F32),
            pltpu.VMEM((HIST * ENT, 128), F32),
            pltpu.VMEM((HIST * ENT, 128), F32),
            pltpu.VMEM((BLOCKS * 8, 128), F32),
            pltpu.VMEM((512, 512), BF16),
            pltpu.VMEM((512, 512), BF16),
            pltpu.VMEM((BLOCKS, 128), F32),
            pltpu.VMEM((32, 128), F32),
            pltpu.VMEM((8, 32, 128), F32),
            pltpu.VMEM((32, 128), F32),
            pltpu.VMEM((16, 32, 128), F32),
            pltpu.VMEM((NF, SLOTS, 128), F32),
            pltpu.VMEM((NF, SLOTS, 128), F32),
            pltpu.VMEM((512, 128), BF16),
            pltpu.VMEM((3, ROWS + 16, 128), F32),
            pltpu.VMEM((1, 128), F32),
            pltpu.VMEM((ND, 1, 128), F32),
            pltpu.VMEM((HIST, 128), F32),
            pltpu.VMEM((NF, SLOTS, 128), BF16),
            pltpu.VMEM((NF, SLOTS, 128), BF16),
            pltpu.VMEM((ENT, 128), F32),
            pltpu.VMEM((ENT, 128), F32),
            pltpu.VMEM((24, BLK + 2 * EDGE, 128), F32),
            pltpu.VMEM((BLOCKS, 16, 128), BF16),
            pltpu.SemaphoreType.DMA((11 + CHUNKS,)),
            pltpu.SemaphoreType.DMA((13,)),
            pltpu.SemaphoreType.DMA((13,)),
        ],
        compiler_params=pltpu.CompilerParams(
            collective_id=0, has_side_effects=True, vmem_limit_bytes=55 << 20
        ),
    )(
        flow, wm, aop, wc.reshape(1, 128), ws.reshape(1, 128), rbf,
        owner.reshape(1, BLOCKS), row.reshape(1, BLOCKS),
        jnp.transpose(disp, (1, 0, 2)), stiff,
        jnp.transpose(vh, (0, 2, 1, 3)).reshape(HIST * ENT, 128),
        jnp.transpose(wh, (0, 2, 1, 3)).reshape(HIST * ENT, 128),
    )
    new_flow, moved, wall_next, norm = pl.pallas_call(
        finish,
        name="wall",
        out_shape=(
            jax.ShapeDtypeStruct((3, POINTS, 128), BF16),
            jax.ShapeDtypeStruct((ENT, 128), F32),
            jax.ShapeDtypeStruct((3, POINTS), F32),
            jax.ShapeDtypeStruct((1, 1), F32),
        ),
        in_specs=[vmem, vmem, vmem, any_, vmem],
        out_specs=(any_,) * 4,
        scratch_shapes=[pltpu.VMEM((3, POINTS), F32), pltpu.SemaphoreType.DMA((9,))],
        compiler_params=pltpu.CompilerParams(vmem_limit_bytes=8 << 20),
    )(*out)
    moved = jnp.transpose(moved.reshape(3, ROWS, 128), (1, 0, 2))
    return new_flow, moved, wall_next, norm.reshape(())


def solution(mesh):
    both = ("fluid", "solid")
    return jax.shard_map(
        per_device,
        mesh=mesh,
        in_specs=(
            P(None, both, None), P(None, both), P(), P(), P(), P(both, None, None), P(both, None), P(both, None),
            P(both, None, None), P(both, None), P(None, both, None, None), P(None, both, None, None),
        ),
        out_specs=(P(None, both, None), P(both, None, None), P(None, both), P()),
        check_vma=False,
    )
```
